32 devices in a mesh: grp: 2 (over y), seq: 16 (over z, x, core).
Axes of the slice: x: 2, y: 2, z: 4, core: 2. Of those that a mesh axis runs over, the one named last changes fastest.
Arguments:
- queries: bfloat16 [8192, 2048], P(('grp', 'seq')), parts along dimension 0, may hold values from -6 to 6
- keys: bfloat16 [8192, 2048], P(('grp', 'seq')), parts along dimension 0, may hold values from -6 to 6
- values: bfloat16 [8192, 2048], P(('grp', 'seq')), parts along dimension 0, may hold values from -6 to 6
- feature_map: bfloat16 [16, 128, 128], replicated, may hold values from -0.5 to 0.5
- out_grad: bfloat16 [8192, 2048], P(('grp', 'seq')), parts along dimension 0, may hold values from -6 to 6
Outputs:
- attended: bfloat16 [8192, 2048], P(('grp', 'seq')), parts along dimension 0
- query_grad: bfloat16 [8192, 2048], P(('grp', 'seq')), parts along dimension 0
- key_grad: bfloat16 [8192, 2048], P(('grp', 'seq')), parts along dimension 0
- value_grad: bfloat16 [8192, 2048], P(('grp', 'seq')), parts along dimension 0
- feature_grad: float32 [524288], P(('grp', 'seq')), parts along dimension 0
The draws below stay inside these ranges and needn't reach their ends.
There are 2 independent parts, one for each index of `grp`. The reference program is written for one: setup_inputs(seed, part) draws one part's arguments, and reference() takes and returns one part's arrays. A program takes and returns all parts, laid end to end along the dimension named above; an argument that names none is the same for every part. Nothing has to cross between parts.
All inputs are finite; a program needn't handle non-finite values.
Results may differ from the reference program's by a relative error of at most 0.0085.
Values may be sent and summed in bfloat16 or wider, within the bound.
A program may use at most 64 MiB of HBM per device.

```python
import math
import jax
import jax.numpy as jnp
from jax import lax

HEADS = 16
DH = 128
TOK_DEV = 256
TOKENS = 4096


def strengthened(array, key, source, target, shards_of, factor):
    def block_of(axis_at):
        return (jnp.arange(array.shape[axis_at]) // (array.shape[axis_at] // shards_of)).reshape((-1,) + (1,) * (array.ndim - 1 - axis_at))

    near = jax.random.permutation(key, shards_of)[block_of(target)]
    far = (block_of(target) + shards_of // 2) % shards_of
    return jnp.where((block_of(source) == near) | (block_of(source) == far), factor * array, array)


def levels(stream_key, extent, split, least, high):
    gain, own = 1.0, jax.random.fold_in(stream_key, 6)
    for axis_at, blocks in split:
        heights = jnp.exp(jax.random.uniform(jax.random.fold_in(own, axis_at), (blocks,), jnp.float32, least / len(split), high / len(split)))
        gain = gain * jnp.repeat(heights, extent[axis_at] // blocks).reshape([-1 if axis == axis_at else 1 for axis in range(len(extent))])
    return gain


def normal_values(stream_key, dims, width, reach, pieces=(), dtype=jnp.bfloat16):
    gain = levels(stream_key, dims, pieces, -0.22, 0.18) if pieces else 1.0
    array = jax.random.normal(stream_key, dims, jnp.float32) * width * gain
    return jnp.minimum(jnp.maximum(array, -reach), reach).astype(dtype)


def gaussian_with(key, shape, spread, most, shards, heavy, held_as=jnp.bfloat16):
    entries = spread * jax.random.normal(key, shape, jnp.float32)
    if shards:
        entries = entries * levels(key, shape, shards, -0.22, 0.18)
    return jnp.clip(strengthened(entries, jax.random.fold_in(key, 3), *heavy), -most, most).astype(held_as)


def setup_inputs(seed: int = 0, part: int = 0) -> dict:
    streams_of = jax.random.split(jax.random.key(seed), 6)
    own_keys = jax.random.split(jax.random.fold_in(streams_of[5], part), 6)
    return {
        "queries": gaussian_with(own_keys[0], (TOKENS, HEADS * DH), 1.0, 6.0, ((0, 16),), (0, 1, 16, 2.0)),
        "keys": normal_values(own_keys[1], (TOKENS, HEADS * DH), 1.0, 6.0, ((0, 16),)),
        "values": normal_values(own_keys[2], (TOKENS, HEADS * DH), 1.0, 6.0, ((0, 16),)),
        "feature_map": normal_values(streams_of[3], (HEADS, DH, DH), DH ** -0.5, 0.5),
        "out_grad": normal_values(own_keys[4], (TOKENS, HEADS * DH), 1.0, 6.0, ((0, 16),)),
    }


def mixing(form, left, right):
    return jnp.einsum(form, left.astype(jnp.float32), right.astype(jnp.float32))

def features(inputs, weight):
    lifted = mixing('thd,hde->the', inputs, weight)
    mapped = jnp.where(lifted > 0, lifted + 1.0, jnp.exp(jnp.minimum(lifted, 0.0)))
    return (lifted, mapped.astype(jnp.bfloat16))

def slope_of(lifted):
    return jnp.where(lifted > 0, 1.0, jnp.exp(jnp.minimum(lifted, 0.0)))

def reference(queries, keys, values, feature_map, out_grad):
    block_count = TOKENS // TOK_DEV
    shaped = (block_count, TOK_DEV, HEADS, DH)
    query_blocks = queries.reshape(shaped)
    key_blocks = keys.reshape(shaped)
    value_blocks = values.reshape(shaped)
    grad_blocks = out_grad.reshape(shaped)
    token_ids = lax.broadcasted_iota(jnp.int32, (TOK_DEV, TOK_DEV), 0)
    other_ids = lax.broadcasted_iota(jnp.int32, (TOK_DEV, TOK_DEV), 1)
    causal = (token_ids >= other_ids)[None, :, :]
    zero_state = jnp.zeros((HEADS, DH, DH), jnp.float32)

    def forward_step(prefix, blocks):
        query_block, key_block, value_block = blocks
        lifted_q, feat_q = features(query_block, feature_map)
        lifted_k, feat_k = features(key_block, feature_map)
        scores = jnp.where(causal, mixing('the,she->hts', feat_q, feat_k), 0.0).astype(jnp.bfloat16)
        numerator = mixing('hts,shf->thf', scores, value_block) + mixing('the,hef->thf', feat_q, prefix.astype(jnp.bfloat16))
        recip = lax.rsqrt(lax.optimization_barrier(jnp.mean(numerator * numerator, axis=-1, keepdims=True)) + 1e-06)
        attended = (numerator * recip).astype(jnp.bfloat16)
        block_state = mixing('the,thf->hef', feat_k, value_block)
        return (prefix + block_state, (attended, prefix))
    last_state, (attended_blocks, prefixes) = lax.scan(forward_step, zero_state, (query_blocks, key_blocks, value_blocks))
    scale = 1.0 / math.sqrt(TOKENS)

    def backward_step(carry, blocks):
        suffix, weight_sum = carry
        query_block, key_block, value_block, grad_block, prefix = blocks
        lifted_q, feat_q = features(query_block, feature_map)
        lifted_k, feat_k = features(key_block, feature_map)
        prefix_low = prefix.astype(jnp.bfloat16)
        suffix_low = suffix.astype(jnp.bfloat16)
        scores = jnp.where(causal, mixing('the,she->hts', feat_q, feat_k), 0.0).astype(jnp.bfloat16)
        numerator = mixing('hts,shf->thf', scores, value_block) + mixing('the,hef->thf', feat_q, prefix_low)
        recip = lax.rsqrt(lax.optimization_barrier(jnp.mean(numerator * numerator, axis=-1, keepdims=True)) + 1e-06)
        upstream = grad_block.astype(jnp.float32)
        inner = lax.optimization_barrier(jnp.mean(upstream * numerator, axis=-1, keepdims=True))
        grad_numer = (recip * (upstream - numerator * recip * recip * inner)).astype(jnp.bfloat16)
        back_scores = jnp.where(causal, mixing('thf,shf->hts', grad_numer, value_block), 0.0).astype(jnp.bfloat16)
        grad_fq = mixing('hts,she->the', back_scores, feat_k) + mixing('thf,hef->the', grad_numer, prefix_low)
        grad_fk = mixing('hts,the->she', back_scores, feat_q) + mixing('shf,hef->she', value_block, suffix_low)
        value_grad = (mixing('hts,thf->shf', scores, grad_numer) + mixing('she,hef->shf', feat_k, suffix_low)).astype(jnp.bfloat16)
        grad_qa = (grad_fq * slope_of(lifted_q)).astype(jnp.bfloat16)
        grad_ka = (grad_fk * slope_of(lifted_k)).astype(jnp.bfloat16)
        query_grad = mixing('the,hde->thd', grad_qa, feature_map).astype(jnp.bfloat16)
        key_grad = mixing('the,hde->thd', grad_ka, feature_map).astype(jnp.bfloat16)
        weight_term = mixing('thd,the->hde', query_block, grad_qa) + mixing('thd,the->hde', key_block, grad_ka)
        local_adjoint = mixing('the,thf->hef', feat_q, grad_numer)
        return ((suffix + local_adjoint, weight_sum + weight_term), (query_grad, key_grad, value_grad))
    carry_end, (query_grads, key_grads, value_grads) = lax.scan(backward_step, (zero_state, zero_state), (query_blocks, key_blocks, value_blocks, grad_blocks, prefixes), reverse=True)
    flat = (TOKENS, HEADS * DH)
    feature_grad = (carry_end[1] * scale).reshape(HEADS * DH * DH)
    return (attended_blocks.reshape(flat), query_grads.reshape(flat), key_grads.reshape(flat), value_grads.reshape(flat), feature_grad)
```

```python
import functools
import math

import jax
import jax.numpy as jnp
from jax import lax
from jax.experimental import pallas as pl
from jax.experimental.pallas import tpu as pltpu
from jax.sharding import PartitionSpec as P

MESH = pl.DeviceIdType.MESH
BF16 = jnp.bfloat16
F32 = jnp.float32
GROUP = 4
PIECES = 1
ORDER = [
    "U0", "U1", "T0", "U2", "T1", "U3", "T2", "L0", "T3", "L1", "S0", "L2", "S1", "L3",
    "S2", "S3", "H0", "H1", "N0", "H2", "N1", "RT0", "H3", "N2", "RT1", "N3", "RT2", "A0",
    "RT3", "A1", "RS0", "A2", "RS1", "A3", "RS2", "RS3", "RH0", "RH1", "K0", "RH2", "K1", "FT0",
    "RH3", "K2", "FT1", "K3", "FT2", "E0", "FT3", "E1", "E2", "E3",
]


def mm(a, b, ca, cb):
    return lax.dot_general(a, b, (((ca,), (cb,)), ((), ())), preferred_element_type=F32)


def group_heads(heads, groups, g):
    size = heads // groups
    if groups == size:
        return [size * z + (g + z) % size for z in range(size)]
    return list(range(g * size, (g + 1) * size))


def kernel(n, heads, dh, groups, scale, q_hbm, k_hbm, v_hbm, w_hbm, y_hbm,
           att_hbm, qg_hbm, kg_hbm, vg_hbm, fg_ref,
           q_ref, k_ref, v_ref, w_ref, y_ref, att_ref, qg_ref, kg_ref, vg_ref,
           fq_s, fk_s, gb_s, a_s, num_s, gfk_s, vgl_s, wt_s, g_s,
           u_send, r_send, p_full, s_full, f_send,
           u_pair, u_tot, u_recv, p_send, p_chip, p_fwd,
           r_pair, r_tot, r_recv, s_send, s_chip, s_fwd,
           f_pair, f_tot, f_recv,
           pair_send_sems, pair_recv_sems, chip_send_sems, chip_recv_sems, load_sems, late_sems, out_sems):
    me = lax.axis_index("seq")
    chips = n // 2
    chip, core = me // 2, lax.rem(me, 2)
    other = 1 - core
    rows = heads * dh // n
    size = heads // groups
    piece = rows // groups
    tokens = q_ref.shape[0]
    per_head = dh // piece // 2
    shares = dh // rows
    members = [group_heads(heads, groups, g) for g in range(groups)]
    batches = [[m[i:i + GROUP] for i in range(0, size, GROUP)] for m in members]
    short = chips <= 8

    def col(h):
        return pl.ds(h * dh, dh)

    def head_loads(g):
        copies = []
        for h in members[g]:
            copies += [
                pltpu.make_async_copy(w_hbm.at[h], w_ref.at[h], load_sems.at[0, h]),
                pltpu.make_async_copy(k_hbm.at[:, col(h)], k_ref.at[:, col(h)], load_sems.at[1, h]),
                pltpu.make_async_copy(v_hbm.at[:, col(h)], v_ref.at[:, col(h)], load_sems.at[2, h]),
            ]
        return copies

    def store(which, h):
        src, dst = ((att_ref, att_hbm), (qg_ref, qg_hbm), (kg_ref, kg_hbm), (vg_ref, vg_hbm))[which]
        return pltpu.make_async_copy(src.at[:, col(h)], dst.at[:, col(h)], out_sems.at[which, h])

    for g in range(groups):
        for copy in head_loads(g):
            copy.start()

    load_q = pltpu.make_async_copy(q_hbm, q_ref, late_sems.at[0])
    load_y = pltpu.make_async_copy(y_hbm, y_ref, late_sems.at[1])
    load_q.start()
    load_y.start()

    barrier = pltpu.get_barrier_semaphore()

    @pl.loop(0, chips - 1)
    def _(i):
        to = 2 * lax.rem(chip + 1 + i, chips) + core
        pl.semaphore_signal(barrier, inc=1, device_id={"seq": to}, device_id_type=MESH)

    pl.semaphore_signal(barrier, inc=1, device_id={"seq": 2 * chip + other}, device_id_type=MESH)

    causal = (lax.broadcasted_iota(jnp.int32, (tokens, tokens), 0)
              >= lax.broadcasted_iota(jnp.int32, (tokens, tokens), 1))

    def to_pair(phase, g, src, dst):
        return pltpu.make_async_remote_copy(
            src_ref=src, dst_ref=dst, send_sem=pair_send_sems.at[phase],
            recv_sem=pair_recv_sems.at[phase, g], device_id={"seq": 2 * chip + other}, device_id_type=MESH)

    def to_chip(phase, g, src, dst, c):
        return pltpu.make_async_remote_copy(
            src_ref=src, dst_ref=dst, send_sem=chip_send_sems.at[phase],
            recv_sem=chip_recv_sems.at[phase, g], device_id={"seq": 2 * c + core}, device_id_type=MESH)

    def send_all(phase, g, src, dst):
        @pl.loop(1, chips, unroll=short)
        def _(i):
            c = lax.rem(chip + i, chips)
            to_chip(phase, g, src.at[g, c], dst.at[g, chip], c).start()

        dst[g, chip] = src[g, chip]

    def wait_all(phase, g, dst):
        some = dst.at[g, pl.ds(0, chips - 1)]
        to_chip(phase, g, some, some, lax.rem(chip + 1, chips)).wait_recv()

    def share(phase, g, full, paired):
        to_pair(phase, g, full.at[g, :, other], paired.at[g]).start()

    def total(phase, chip_phase, g, full, paired, tot, recv):
        to_pair(phase, g, paired.at[g], paired.at[g]).wait_recv()
        tot[g] = (full[g, :, core].astype(F32) + paired[g].astype(F32)).astype(BF16)
        send_all(chip_phase, g, tot, recv)

    def scan(phase, next_phase, g, recv, send, landing, order):
        wait_all(phase, g, recv)

        def step(i, acc):
            c = order(i)
            send[g, c] = acc.astype(BF16)
            return acc + recv[g, c].astype(F32)

        lax.fori_loop(0, chips, step, jnp.zeros((piece, dh), F32), unroll=short)
        send_all(next_phase, g, send, landing)

    def hand_out(chip_phase, phase, g, landing, full, paired, fwd, out, own_adds):
        wait_all(chip_phase, g, landing)
        base = landing[g].astype(F32)
        theirs = base + jnp.where(own_adds, 0.0, full[g, :, core].astype(F32))
        fwd[g] = theirs.astype(BF16)
        to_pair(phase, g, fwd.at[g], out.at[g, :, core]).start()
        mine = base + jnp.where(own_adds, paired[g].astype(F32), 0.0)
        out[g, :, core] = mine.astype(BF16)

    def receive(phase, g, fwd, out):
        to_pair(phase, g, fwd.at[g], out.at[g, :, other]).wait_recv()

    def put_head(buf, g, k, value):
        buf[g, k * per_head:(k + 1) * per_head] = value.astype(BF16).reshape(per_head, 2, piece, dh)

    def get_head(buf, g, k):
        return buf[g, k * per_head:(k + 1) * per_head].reshape(dh, dh)

    def features(lifted):
        return jnp.where(lifted > 0, lifted + 1.0, jnp.exp(jnp.minimum(lifted, 0.0))).astype(BF16)

    def slope_of(feat):
        return jnp.minimum(feat.astype(F32), 1.0)

    def batched(step):
        def run(g):
            for b, hs in enumerate(batches[g]):
                step(g, b * GROUP, hs)
        return run

    @batched
    def state(g, at, hs):
        lifted = [mm(k_ref[:, col(h)], w_ref[h], 1, 0) for h in hs]
        feats = [features(x) for x in lifted]
        sums = [mm(f, v_ref[:, col(h)], 0, 0) for h, f in zip(hs, feats)]
        for k, h in enumerate(hs):
            fk_s[:, col(h)] = feats[k]
            put_head(u_send, g, at + k, sums[k])

    @batched
    def local_part(g, at, hs):
        lifted = [mm(q_ref[:, col(h)], w_ref[h], 1, 0) for h in hs]
        feats = [features(x) for x in lifted]
        scores = [mm(f, fk_s[:, col(h)], 1, 1) for h, f in zip(hs, feats)]
        scores = [jnp.where(causal, x, 0.0).astype(BF16) for x in scores]
        nums = [mm(x, v_ref[:, col(h)], 1, 0) for h, x in zip(hs, scores)]
        for k, h in enumerate(hs):
            fq_s[:, col(h)] = feats[k]
            a_s[h] = scores[k]
            num_s[:, col(h)] = nums[k]

    @batched
    def numerators(g, at, hs):
        prefixes = [get_head(p_full, g, at + k) for k in range(len(hs))]
        fqs = [fq_s[:, col(h)] for h in hs]
        nums = [num_s[:, col(h)] + mm(f, p, 1, 0) for h, f, p in zip(hs, fqs, prefixes)]
        recips = [lax.rsqrt(jnp.mean(x * x, axis=-1, keepdims=True) + 1e-06) for x in nums]
        ys = [y_ref[:, col(h)].astype(F32) for h in hs]
        inners = [jnp.mean(y * x, axis=-1, keepdims=True) for y, x in zip(ys, nums)]
        grads = [(r * (y - x * (r * r * m))).astype(BF16) for r, y, x, m in zip(recips, ys, nums, inners)]
        sums = [mm(f, x, 0, 0) for f, x in zip(fqs, grads)]
        for k, h in enumerate(hs):
            put_head(r_send, g, at + k, sums[k])
            att_ref[:, col(h)] = (nums[k] * recips[k]).astype(BF16)
            g_s[:, col(h)] = grads[k]

    @batched
    def adjoint_part(g, at, hs):
        grads = [g_s[:, col(h)] for h in hs]
        prefixes = [get_head(p_full, g, at + k) for k in range(len(hs))]
        backs = [mm(x, v_ref[:, col(h)], 1, 1) for x, h in zip(grads, hs)]
        backs = [jnp.where(causal, x, 0.0).astype(BF16) for x in backs]
        gfqs = [mm(b, fk_s[:, col(h)], 1, 0) + mm(x, p, 1, 1) for b, h, x, p in zip(backs, hs, grads, prefixes)]
        fqs = [fq_s[:, col(h)] for h in hs]
        gas = [(x * slope_of(f)).astype(BF16) for x, f in zip(gfqs, fqs)]
        qgs = [mm(x, w_ref[h], 1, 1).astype(BF16) for x, h in zip(gas, hs)]
        wts = [mm(q_ref[:, col(h)], x, 0, 0) for h, x in zip(hs, gas)]
        gfks = [mm(b, f, 0, 0) for b, f in zip(backs, fqs)]
        vgls = [mm(a_s[h], x, 0, 0) for h, x in zip(hs, grads)]
        for k, h in enumerate(hs):
            qg_ref[:, col(h)] = qgs[k]
            wt_s[h] = wts[k]
            gfk_s[:, col(h)] = gfks[k]
            vgl_s[:, col(h)] = vgls[k]

    def place(h, b):
        d = h * shares + b
        return d // 2, d % 2

    homes = []
    for g in range(groups):
        of_core = ([], [])
        for k, h in enumerate(members[g]):
            for b in range(shares):
                c, parity = place(h, b)
                of_core[parity].append((c, k, b))
        homes.append(of_core)

    @batched
    def key_part(g, at, hs):
        suffixes = [get_head(s_full, g, at + k) for k in range(len(hs))]
        fks = [fk_s[:, col(h)] for h in hs]
        gfks = [gfk_s[:, col(h)] + mm(v_ref[:, col(h)], s, 1, 1) for h, s in zip(hs, suffixes)]
        gbs = [(x * slope_of(f)).astype(BF16) for x, f in zip(gfks, fks)]
        wts = [wt_s[h] + mm(k_ref[:, col(h)], x, 0, 0) for h, x in zip(hs, gbs)]
        for k, h in enumerate(hs):
            gb_s[:, col(h)] = gbs[k]
        for parity in range(2):
            for j, (_, k, b) in enumerate(homes[g][parity]):
                if at <= k < at + len(hs):
                    f_send[g, parity, j] = wts[k - at][b * rows:(b + 1) * rows].astype(BF16)

    def share_weights(g):
        to_pair(4, g, f_send.at[g, other], f_pair.at[g]).start()

    def total_weights(g):
        to_pair(4, g, f_pair.at[g], f_pair.at[g]).wait_recv()
        f_tot[g] = (f_send[g, core].astype(F32) + f_pair[g].astype(F32)).astype(BF16)
        for j, ((c0, _, _), (c1, _, _)) in enumerate(zip(*homes[g])):
            c = c0 + core * (c1 - c0)

            @pl.when(c != chip)
            def _():
                pltpu.make_async_remote_copy(
                    src_ref=f_tot.at[g, j], dst_ref=f_recv.at[chip], send_sem=chip_send_sems.at[4],
                    recv_sem=chip_recv_sems.at[4, 0], device_id={"seq": 2 * c + core}, device_id_type=MESH).start()

            @pl.when(c == chip)
            def _():
                f_recv[chip] = f_tot[g, j]

    @batched
    def last_part(g, at, hs):
        suffixes = [get_head(s_full, g, at + k) for k in range(len(hs))]
        vgs = [vgl_s[:, col(h)] + mm(fk_s[:, col(h)], s, 1, 0) for h, s in zip(hs, suffixes)]
        kgs = [mm(gb_s[:, col(h)], w_ref[h], 1, 1) for h in hs]
        for h, a, b in zip(hs, vgs, kgs):
            vg_ref[:, col(h)] = a.astype(BF16)
            kg_ref[:, col(h)] = b.astype(BF16)

    def put_out(which, g):
        for h in members[g]:
            store(which, h).start()

    class Steps:
        def U(g):
            for copy in head_loads(g):
                copy.wait()
            state(g)
            if g == 0:
                pl.semaphore_wait(barrier, chips)
            share(0, g, u_send, u_pair)

        def T(g):
            total(0, 0, g, u_send, u_pair, u_tot, u_recv)

        def L(g):
            if g == 0:
                load_q.wait()
            local_part(g)

        def S(g):
            scan(0, 1, g, u_recv, p_send, p_chip, lambda i: i)

        def H(g):
            hand_out(1, 1, g, p_chip, u_send, u_pair, p_fwd, p_full, core == 1)

        def N(g):
            if g == 0:
                load_y.wait()
            receive(1, g, p_fwd, p_full)
            numerators(g)
            share(2, g, r_send, r_pair)
            put_out(0, g)

        def RT(g):
            total(2, 2, g, r_send, r_pair, r_tot, r_recv)

        def A(g):
            adjoint_part(g)
            put_out(1, g)

        def RS(g):
            scan(2, 3, g, r_recv, s_send, s_chip, lambda i: chips - 1 - i)

        def RH(g):
            hand_out(3, 3, g, s_chip, r_send, r_pair, s_fwd, s_full, core == 0)

        def K(g):
            receive(3, g, s_fwd, s_full)
            key_part(g)
            share_weights(g)

        def FT(g):
            total_weights(g)

        def E(g):
            last_part(g)
            put_out(2, g)
            put_out(3, g)

    for step in ORDER:
        name, g = step[:-1], int(step[-1])
        if g < groups:
            getattr(Steps, name)(g)

    some = f_recv.at[pl.ds(0, chips - 1)]
    to_chip(4, 0, some, some, lax.rem(chip + 1, chips)).wait_recv()

    def collect(c, acc):
        return acc + f_recv[c].astype(F32)

    fg_ref[...] = lax.fori_loop(0, chips, collect, jnp.zeros((rows, dh), F32), unroll=short) * scale

    for which in range(4):
        for h in range(heads):
            store(which, h).wait()

    for phase, buf in enumerate((u_tot, p_send, r_tot, s_send)):
        sent = buf.at[:, pl.ds(0, chips - 1)]
        to_chip(phase, 0, sent, sent, lax.rem(chip + 1, chips)).wait_send()
    to_chip(4, 0, some, some, lax.rem(chip + 1, chips)).wait_send()
    for phase, buf in enumerate((u_pair, p_fwd, r_pair, s_fwd, f_pair)):
        to_pair(phase, 0, buf, buf).wait_send()


def copy_out(*refs):
    ins, outs, held = refs[:5], refs[5:10], refs[10:15]
    in_sems, out_sems = refs[15:]

    def parts(sources, targets, sems):
        copies = []
        for i, (source, target) in enumerate(zip(sources, targets)):
            size = source.shape[0] // PIECES
            for p in range(PIECES):
                some = pl.ds(p * size, size)
                copies.append(pltpu.make_async_copy(source.at[some], target.at[some], sems.at[i, p]))
        return copies

    reads = parts(ins, held, in_sems)
    writes = parts(held, outs, out_sems)
    for read in reads:
        read.start()
    for read, write in zip(reads, writes):
        read.wait()
        write.start()
    for write in writes:
        write.wait()


def local(queries, keys, values, feature_map, out_grad):
    tokens, width = queries.shape
    heads, dh, _ = feature_map.shape
    n = lax.axis_size("seq")
    chips, rows = n // 2, heads * dh // n
    groups = max(1, min(4, rows // 16))
    piece = rows // groups
    kinds = [pltpu.VMEM((groups, chips, 2, piece, dh), BF16)] * 4
    parts = [pltpu.VMEM((groups, chips, piece, dh), BF16)] * 12
    taken = chips // groups
    wide = jax.ShapeDtypeStruct((tokens, width), BF16)
    vmem = pl.BlockSpec(memory_space=pltpu.VMEM)
    hbm = pl.BlockSpec(memory_space=pltpu.HBM)
    shapes = (wide, wide, wide, wide, jax.ShapeDtypeStruct((rows, dh), F32))
    outs = pl.pallas_call(
        functools.partial(kernel, n, heads, dh, groups, 1.0 / math.sqrt(tokens * n)),
        out_shape=shapes,
        in_specs=[hbm] * 5,
        out_specs=(hbm,) * 4 + (vmem,),
        scratch_shapes=[pltpu.VMEM((tokens, width), BF16)] * 3 + [pltpu.VMEM((heads, dh, dh), BF16)] + [
            pltpu.VMEM((tokens, width), BF16)] * 8 + [
            pltpu.VMEM((heads, tokens, tokens), BF16),
            pltpu.VMEM((tokens, width), F32),
            pltpu.VMEM((tokens, width), F32),
            pltpu.VMEM((tokens, width), F32),
            pltpu.VMEM((heads, dh, dh), F32),
            pltpu.VMEM((tokens, width), BF16),
        ] + kinds + [pltpu.VMEM((groups, 2, taken, rows, dh), BF16)] + parts + [
            pltpu.VMEM((groups, taken, rows, dh), BF16),
            pltpu.VMEM((groups, taken, rows, dh), BF16),
            pltpu.VMEM((chips, rows, dh), BF16),
            pltpu.SemaphoreType.DMA((5,)),
            pltpu.SemaphoreType.DMA((5, groups)),
            pltpu.SemaphoreType.DMA((5,)),
            pltpu.SemaphoreType.DMA((5, groups)),
            pltpu.SemaphoreType.DMA((3, heads)),
            pltpu.SemaphoreType.DMA((2,)),
            pltpu.SemaphoreType.DMA((4, heads)),
        ],
        compiler_params=pltpu.CompilerParams(
            collective_id=0, has_side_effects=True, vmem_limit_bytes=56 << 20),
        name="linear_attention",
    )(queries, keys, values, feature_map, out_grad)
    outs = pl.pallas_call(
        copy_out,
        out_shape=shapes,
        in_specs=[hbm] * 5,
        out_specs=(hbm,) * 5,
        scratch_shapes=[pltpu.VMEM(x.shape, x.dtype) for x in shapes] + [pltpu.SemaphoreType.DMA((5, PIECES))] * 2,
        compiler_params=pltpu.CompilerParams(vmem_limit_bytes=56 << 20),
        name="copy_out",
    )(*outs)
    return tuple(outs[:4]) + (outs[4].reshape(rows * dh),)


def solution(mesh):
    wide = P(("grp", "seq"), None)
    return jax.shard_map(
        local, mesh=mesh, in_specs=(wide, wide, wide, P(), wide),
        out_specs=(wide, wide, wide, wide, P(("grp", "seq"))), check_vma=False)
```

```python
import functools
import math

import jax
import jax.numpy as jnp
from jax import lax
from jax.experimental import pallas as pl
from jax.experimental.pallas import tpu as pltpu
from jax.sharding import PartitionSpec as P

MESH = pl.DeviceIdType.MESH
BF16 = jnp.bfloat16
F32 = jnp.float32
GROUPS = 4
PIECES = 1
ORDER = [
    "U0", "U1", "U2", "U3", "L0", "L1", "S0", "L2", "S1", "L3", "S2", "S3", "N0", "N1",
    "N2", "N3", "A0", "A1", "RS0", "A2", "RS1", "A3", "RS2", "RS3", "K0", "K1", "K2", "K3",
    "E0", "E1", "E2", "E3",
]


def mm(a, b, ca, cb):
    return lax.dot_general(a, b, (((ca,), (cb,)), ((), ())), preferred_element_type=F32)


def kernel(n, heads, dh, groups, scale, q_hbm, k_hbm, v_hbm, w_hbm, y_hbm,
           att_hbm, qg_hbm, kg_hbm, vg_hbm, fg_ref,
           q_ref, k_ref, v_ref, y_ref, att_ref, qg_ref, kg_ref, vg_ref, fq_s, fk_s, gb_s, g_s,
           num_s, gfk_s, vgl_s, a_s, w_ref, p_late, s_late, wt_s, u_first, r_last,
           u_tot, p_chip, r_tot, s_chip, u_recv, p_send, r_recv, s_send,
           f_tot, f_pair, f_recv,
           load_sems, give_sems, take_sems, out_sems, out_give_sems, out_take_sems,
           chip_send_sems, chip_recv_sems, f_pair_sems):
    me = lax.axis_index("seq")
    chips = n // 2
    chip, core = me // 2, lax.rem(me, 2)
    other = 1 - core
    rows = heads * dh // n
    held = heads // 2
    owners, first_owner = chips // 2, chips // 4
    is_owner = (chip >= first_owner) & (chip < first_owner + owners)
    place = chip - first_owner
    tokens = q_hbm.shape[0]
    piece = p_chip.shape[2]
    per_head = dh // piece
    shares = dh // rows
    members = [list(range(g, held, groups)) for g in range(groups)]
    short = chips <= 8
    blocks = [pl.ds(0, tokens), pl.ds(tokens, tokens)]
    ours = pl.ds(pl.multiple_of(core * tokens, tokens), tokens)
    theirs = pl.ds(pl.multiple_of(other * tokens, tokens), tokens)

    def col(j):
        return pl.ds(j * dh, dh)

    def wide(j, parity):
        return pl.ds(pl.multiple_of((2 * j + parity) * dh, dh), dh)

    inputs = ((k_hbm, k_ref), (v_hbm, v_ref), (q_hbm, q_ref), (y_hbm, y_ref))

    def load(a, j):
        src, dst = inputs[a]
        return pltpu.make_async_copy(src.at[:, wide(j, core)], dst.at[ours, col(j)], load_sems.at[a, j])

    def load_map(j):
        return pltpu.make_async_copy(w_hbm.at[2 * j + core], w_ref.at[j], load_sems.at[4, j])

    def to_pair(src, dst, send_sem, recv_sem):
        return pltpu.make_async_remote_copy(
            src_ref=src, dst_ref=dst, send_sem=send_sem, recv_sem=recv_sem,
            device_id={"seq": 2 * chip + other}, device_id_type=MESH)

    def give(a, j):
        src, dst = inputs[a]
        return to_pair(src.at[:, wide(j, other)], dst.at[ours, col(j)], give_sems.at[a], take_sems.at[a, j])

    def ready(a, g):
        for j in members[g]:
            load(a, j).wait()
            give(a, j).wait_recv()

    results = ((att_ref, att_hbm), (qg_ref, qg_hbm), (kg_ref, kg_hbm), (vg_ref, vg_hbm))

    def store(which, j):
        src, dst = results[which]
        return pltpu.make_async_copy(src.at[ours, col(j)], dst.at[:, wide(j, core)], out_sems.at[which, j])

    def give_out(which, j):
        src, dst = results[which]
        return to_pair(src.at[theirs, col(j)], dst.at[:, wide(j, core)], out_give_sems.at[which], out_take_sems.at[which])

    def put_out(which, g):
        for j in members[g]:
            store(which, j).start()
            give_out(which, j).start()

    barrier = pltpu.get_barrier_semaphore()
    pl.semaphore_signal(barrier, inc=1, device_id={"seq": 2 * chip + other}, device_id_type=MESH)

    @pl.when(is_owner)
    def _():
        @pl.loop(1, chips)
        def _(i):
            to = 2 * lax.rem(chip + i, chips) + core
            pl.semaphore_signal(barrier, inc=1, device_id={"seq": to}, device_id_type=MESH)

    for g in range(groups):
        for j in members[g]:
            load_map(j).start()
            load(0, j).start()
            load(1, j).start()
    for j in range(held):
        load(2, j).start()
        load(3, j).start()

    causal = (lax.broadcasted_iota(jnp.int32, (tokens, tokens), 0)
              >= lax.broadcasted_iota(jnp.int32, (tokens, tokens), 1))

    def to_chip(phase, g, src, dst, c):
        return pltpu.make_async_remote_copy(
            src_ref=src, dst_ref=dst, send_sem=chip_send_sems.at[phase],
            recv_sem=chip_recv_sems.at[phase, g], device_id={"seq": 2 * c + core}, device_id_type=MESH)

    def some_chip():
        return lax.rem(chip + 1, chips)

    def to_owners(phase, g, tot, recv):
        @pl.loop(0, owners, unroll=short)
        def _(i):
            at = lax.rem(chip + i, owners)
            c = first_owner + at

            @pl.when(c != chip)
            def _():
                to_chip(phase, g, tot.at[g, at], recv.at[g, chip], c).start()

            @pl.when(c == chip)
            def _():
                recv[g, chip] = tot[g, at]

    def scan(phase, g, recv, send, landing, order):
        @pl.when(is_owner)
        def _():
            sent = recv.at[g, pl.ds(0, chips - 1)]
            to_chip(phase, g, sent, sent, some_chip()).wait_recv()

            def step(i, acc):
                c = order(i)
                send[g, c] = acc.astype(BF16)
                return acc + recv[g, c].astype(F32)

            lax.fori_loop(0, chips, step, jnp.zeros((piece, dh), F32), unroll=short)

            @pl.loop(1, chips, unroll=short)
            def _(i):
                c = lax.rem(chip + i, chips)
                to_chip(phase + 1, g, send.at[g, c], landing.at[g, place], c).start()

            landing[g, place] = send[g, chip]

    def arrive(phase, g, landing):
        @pl.when(is_owner)
        def _():
            sent = landing.at[g, pl.ds(0, owners - 1)]
            to_chip(phase, g, sent, sent, some_chip()).wait_recv()

        @pl.when(jnp.logical_not(is_owner))
        def _():
            to_chip(phase, g, landing.at[g], landing.at[g], some_chip()).wait_recv()

    def put_head(buf, g, k, value):
        buf[g, k * per_head:(k + 1) * per_head] = value.astype(BF16).reshape(per_head, piece, dh)

    def get_head(buf, g, k):
        return buf[g, k * per_head:(k + 1) * per_head].reshape(dh, dh)

    def features(lifted):
        return jnp.where(lifted > 0, lifted + 1.0, jnp.exp(jnp.minimum(lifted, 0.0))).astype(BF16)

    def slope_of(feat):
        return jnp.minimum(feat.astype(F32), 1.0)

    def units(g):
        return [(k, j, b) for k, j in enumerate(members[g]) for b in range(2)]

    def state(g):
        js = members[g]
        lifted = [mm(k_ref[:, col(j)], w_ref[j], 1, 0) for j in js]
        feats = [features(x) for x in lifted]
        sums = [[mm(f[b * tokens:(b + 1) * tokens], v_ref[blocks[b], col(j)], 0, 0) for b in range(2)]
                for j, f in zip(js, feats)]
        for k, j in enumerate(js):
            put_head(u_tot, g, k, sums[k][0] + sums[k][1])
            u_first[j] = sums[k][0]
            fk_s[:, col(j)] = feats[k]

    def local_part(g):
        js = members[g]
        lifted = [mm(q_ref[:, col(j)], w_ref[j], 1, 0) for j in js]
        feats = [features(x) for x in lifted]
        scores = [mm(feats[k][b * tokens:(b + 1) * tokens], fk_s[blocks[b], col(j)], 1, 1) for k, j, b in units(g)]
        scores = [jnp.where(causal, x, 0.0).astype(BF16) for x in scores]
        nums = [mm(x, v_ref[blocks[b], col(j)], 1, 0) for (k, j, b), x in zip(units(g), scores)]
        for k, j in enumerate(js):
            fq_s[:, col(j)] = feats[k]
        for (k, j, b), x, a in zip(units(g), nums, scores):
            a_s[2 * j + b] = a
            num_s[blocks[b], col(j)] = x

    def numerators(g):
        for k, j in enumerate(members[g]):
            p_late[j] = (get_head(p_chip, g, k).astype(F32) + u_first[j]).astype(BF16)
        prefixes = [p_late[j] if b else get_head(p_chip, g, k) for k, j, b in units(g)]
        fqs = [fq_s[blocks[b], col(j)] for k, j, b in units(g)]
        nums = [num_s[blocks[b], col(j)] + mm(f, p, 1, 0) for (k, j, b), f, p in zip(units(g), fqs, prefixes)]
        recips = [lax.rsqrt(jnp.mean(x * x, axis=-1, keepdims=True) + 1e-06) for x in nums]
        ys = [y_ref[blocks[b], col(j)].astype(F32) for k, j, b in units(g)]
        inners = [jnp.mean(y * x, axis=-1, keepdims=True) for y, x in zip(ys, nums)]
        grads = [(r * (y - x * (r * r * m))).astype(BF16) for r, y, x, m in zip(recips, ys, nums, inners)]
        sums = [mm(f, x, 0, 0) for f, x in zip(fqs, grads)]
        for k, j in enumerate(members[g]):
            put_head(r_tot, g, k, sums[2 * k] + sums[2 * k + 1])
            r_last[j] = sums[2 * k + 1]
        for (k, j, b), x, r, gr in zip(units(g), nums, recips, grads):
            att_ref[blocks[b], col(j)] = (x * r).astype(BF16)
            g_s[blocks[b], col(j)] = gr

    def adjoint_part(g):
        us = units(g)
        grads = [g_s[blocks[b], col(j)] for k, j, b in us]
        prefixes = [p_late[j] if b else get_head(p_chip, g, k) for k, j, b in us]
        backs = [mm(x, v_ref[blocks[b], col(j)], 1, 1) for x, (k, j, b) in zip(grads, us)]
        backs = [jnp.where(causal, x, 0.0).astype(BF16) for x in backs]
        gfqs = [mm(s, fk_s[blocks[b], col(j)], 1, 0) + mm(x, p, 1, 1)
                for s, (k, j, b), x, p in zip(backs, us, grads, prefixes)]
        fqs = [fq_s[blocks[b], col(j)] for k, j, b in us]
        gas = [(x * slope_of(f)).astype(BF16) for x, f in zip(gfqs, fqs)]
        qgs = [mm(x, w_ref[j], 1, 1).astype(BF16) for x, (k, j, b) in zip(gas, us)]
        wts = [mm(q_ref[blocks[b], col(j)], x, 0, 0) for x, (k, j, b) in zip(gas, us)]
        gfks = [mm(s, f, 0, 0) for s, f in zip(backs, fqs)]
        vgls = [mm(a_s[2 * j + b], x, 0, 0) for x, (k, j, b) in zip(grads, us)]
        for i, (k, j, b) in enumerate(us):
            qg_ref[blocks[b], col(j)] = qgs[i]
            gfk_s[blocks[b], col(j)] = gfks[i]
            vgl_s[blocks[b], col(j)] = vgls[i]
        for k, j in enumerate(members[g]):
            wt_s[j] = wts[2 * k] + wts[2 * k + 1]

    def key_part(g):
        for k, j in enumerate(members[g]):
            s_late[j] = (get_head(s_chip, g, k).astype(F32) + r_last[j]).astype(BF16)
        us = units(g)
        suffixes = [get_head(s_chip, g, k) if b else s_late[j] for k, j, b in us]
        gfks = [gfk_s[blocks[b], col(j)] + mm(v_ref[blocks[b], col(j)], s, 1, 1) for (k, j, b), s in zip(us, suffixes)]
        gbs = [(x * slope_of(fk_s[blocks[b], col(j)])).astype(BF16) for x, (k, j, b) in zip(gfks, us)]
        wts = [mm(k_ref[blocks[b], col(j)], x, 0, 0) for (k, j, b), x in zip(us, gbs)]
        for (k, j, b), x in zip(us, gbs):
            gb_s[blocks[b], col(j)] = x
        for k, j in enumerate(members[g]):
            whole = (wt_s[j] + (wts[2 * k] + wts[2 * k + 1])).astype(BF16)
            if shares == 1:
                f_tot[0, j] = whole
            else:
                for b in range(shares):
                    f_tot[b % 2, j * (shares // 2) + b // 2] = whole[b * rows:(b + 1) * rows]

    def send_rows(src, c):
        @pl.when(c != chip)
        def _():
            to_chip(4, 0, src, f_recv.at[chip], c).start()

        @pl.when(c == chip)
        def _():
            f_recv[chip] = src[...]

    def swap():
        return to_pair(f_tot.at[other], f_pair, f_pair_sems.at[0], f_pair_sems.at[1])

    def send_weights(g):
        if shares == 1:
            for j in members[g]:
                send_rows(f_tot.at[0, j], j)
        elif g == groups - 1:
            swap().start()
            swap().wait_recv()

            @pl.loop(0, held)
            def _(j):
                @pl.loop(0, shares // 2)
                def _(r):
                    at = j * (shares // 2) + r
                    send_rows(f_tot.at[core, at], (2 * j + core) * (shares // 2) + r)
                    send_rows(f_pair.at[at], (2 * j + other) * (shares // 2) + r)

    def last_part(g):
        us = units(g)
        suffixes = [get_head(s_chip, g, k) if b else s_late[j] for k, j, b in us]
        vgs = [vgl_s[blocks[b], col(j)] + mm(fk_s[blocks[b], col(j)], s, 1, 0) for (k, j, b), s in zip(us, suffixes)]
        kgs = [mm(gb_s[:, col(j)], w_ref[j], 1, 1) for j in members[g]]
        for (k, j, b), x in zip(us, vgs):
            vg_ref[blocks[b], col(j)] = x.astype(BF16)
        for k, j in enumerate(members[g]):
            kg_ref[:, col(j)] = kgs[k].astype(BF16)

    class Steps:
        def U(g):
            if g == 0:
                pl.semaphore_wait(barrier, jnp.where(is_owner, owners, owners + 1))
                for i in range(groups):
                    for j in members[i]:
                        give(0, j).start()
                        give(1, j).start()
            for j in members[g]:
                load_map(j).wait()
            ready(0, g)
            ready(1, g)
            state(g)
            to_owners(0, g, u_tot, u_recv)
            if g == 0:
                for j in range(held):
                    give(2, j).start()
            if g == groups - 1:
                for j in range(held):
                    give(3, j).start()

        def L(g):
            ready(2, g)
            local_part(g)

        def S(g):
            scan(0, g, u_recv, p_send, p_chip, lambda i: i)

        def N(g):
            ready(3, g)
            arrive(1, g, p_chip)
            numerators(g)
            to_owners(2, g, r_tot, r_recv)
            put_out(0, g)

        def A(g):
            adjoint_part(g)
            put_out(1, g)

        def RS(g):
            scan(2, g, r_recv, s_send, s_chip, lambda i: chips - 1 - i)

        def K(g):
            arrive(3, g, s_chip)
            key_part(g)
            send_weights(g)

        def E(g):
            last_part(g)
            put_out(2, g)
            put_out(3, g)

    for step in ORDER:
        name, g = step[:-1], int(step[-1])
        if g < groups:
            getattr(Steps, name)(g)

    some = f_recv.at[pl.ds(0, chips - 1)]
    to_chip(4, 0, some, some, some_chip()).wait_recv()

    def collect(c, acc):
        return acc + f_recv[c].astype(F32)

    fg_ref[...] = lax.fori_loop(0, chips, collect, jnp.zeros((rows, dh), F32), unroll=short) * scale

    for which in range(4):
        for j in range(held):
            store(which, j).wait()
        block = results[which][0].at[pl.ds(0, tokens)]
        both = to_pair(block, block, out_give_sems.at[which], out_take_sems.at[which])
        both.wait_send()
        both.wait_recv()
        to_pair(block, block, give_sems.at[which], out_take_sems.at[which]).wait_send()

    @pl.when(is_owner)
    def _():
        for phase, tot, send in ((0, u_tot, p_send), (2, r_tot, s_send)):
            sent = tot.at[:, pl.ds(0, owners - 1)]
            to_chip(phase, 0, sent, sent, some_chip()).wait_send()
            sent = send.at[:, pl.ds(0, chips - 1)]
            to_chip(phase + 1, 0, sent, sent, some_chip()).wait_send()

    @pl.when(jnp.logical_not(is_owner))
    def _():
        for phase, tot in ((0, u_tot), (2, r_tot)):
            to_chip(phase, 0, tot, tot, some_chip()).wait_send()

    to_chip(4, 0, some, some, some_chip()).wait_send()
    if shares > 1:
        swap().wait_send()


def copy_out(*refs):
    ins, outs, held = refs[:5], refs[5:10], refs[10:15]
    in_sems, out_sems = refs[15:]

    def parts(sources, targets, sems):
        copies = []
        for i, (source, target) in enumerate(zip(sources, targets)):
            size = source.shape[0] // PIECES
            for p in range(PIECES):
                some = pl.ds(p * size, size)
                copies.append(pltpu.make_async_copy(source.at[some], target.at[some], sems.at[i, p]))
        return copies

    reads = parts(ins, held, in_sems)
    writes = parts(held, outs, out_sems)
    for read in reads:
        read.start()
    for read, write in zip(reads, writes):
        read.wait()
        write.start()
    for write in writes:
        write.wait()


def local(queries, keys, values, feature_map, out_grad):
    tokens, width = queries.shape
    heads, dh, _ = feature_map.shape
    n = lax.axis_size("seq")
    chips, rows, held = n // 2, heads * dh // n, heads // 2
    owners = chips // 2
    groups = max(1, min(GROUPS, held * dh // (owners * 16)))
    piece = held // groups * dh // owners
    slots = held * max(2, dh // rows) // 2
    wide = jax.ShapeDtypeStruct((tokens, width), BF16)
    vmem = pl.BlockSpec(memory_space=pltpu.VMEM)
    hbm = pl.BlockSpec(memory_space=pltpu.HBM)
    shapes = (wide, wide, wide, wide, jax.ShapeDtypeStruct((rows, dh), F32))
    outs = pl.pallas_call(
        functools.partial(kernel, n, heads, dh, groups, 1.0 / math.sqrt(tokens * n)),
        out_shape=shapes,
        in_specs=[hbm] * 5,
        out_specs=(hbm,) * 4 + (vmem,),
        scratch_shapes=[pltpu.VMEM((2 * tokens, width // 2), BF16)] * 12 + [
            pltpu.VMEM((2 * tokens, width // 2), F32)] * 3 + [
            pltpu.VMEM((heads, tokens, tokens), BF16)] + [
            pltpu.VMEM((held, dh, dh), BF16)] * 3 + [
            pltpu.VMEM((held, dh, dh), F32)] * 3 + [
            pltpu.VMEM((groups, owners, piece, dh), BF16)] * 4 + [
            pltpu.VMEM((groups, chips, piece, dh), BF16)] * 4 + [
            pltpu.VMEM((2, slots, rows, dh), BF16),
            pltpu.VMEM((slots, rows, dh), BF16),
            pltpu.VMEM((chips, rows, dh), BF16),
            pltpu.SemaphoreType.DMA((5, held)),
            pltpu.SemaphoreType.DMA((4,)),
            pltpu.SemaphoreType.DMA((4, held)),
            pltpu.SemaphoreType.DMA((4, held)),
            pltpu.SemaphoreType.DMA((4,)),
            pltpu.SemaphoreType.DMA((4,)),
            pltpu.SemaphoreType.DMA((5,)),
            pltpu.SemaphoreType.DMA((5, groups)),
            pltpu.SemaphoreType.DMA((2,)),
        ],
        compiler_params=pltpu.CompilerParams(
            collective_id=0, has_side_effects=True, vmem_limit_bytes=56 << 20),
        name="linear_attention",
    )(queries, keys, values, feature_map, out_grad)
    outs = pl.pallas_call(
        copy_out,
        out_shape=shapes,
        in_specs=[hbm] * 5,
        out_specs=(hbm,) * 5,
        scratch_shapes=[pltpu.VMEM(x.shape, x.dtype) for x in shapes] + [pltpu.SemaphoreType.DMA((5, PIECES))] * 2,
        compiler_params=pltpu.CompilerParams(vmem_limit_bytes=56 << 20),
        name="copy_out",
    )(*outs)
    return tuple(outs[:4]) + (outs[4].reshape(rows * dh),)


def solution(mesh):
    wide = P(("grp", "seq"), None)
    return jax.shard_map(
        local, mesh=mesh, in_specs=(wide, wide, wide, P(), wide),
        out_specs=(wide, wide, wide, wide, P(("grp", "seq"))), check_vma=False)
```

```python
import functools
import math

import jax
import jax.numpy as jnp
from jax import lax
from jax.experimental import pallas as pl
from jax.experimental.pallas import tpu as pltpu
from jax.sharding import PartitionSpec as P

MESH = pl.DeviceIdType.MESH
BF16 = jnp.bfloat16
F32 = jnp.float32
GROUPS = 4
DIRECT = (2, 3, 1,)
ORDER = [
    "U0", "U1", "U2", "U3", "L0", "L1", "S0", "L2", "S1", "L3", "S2", "S3", "N0", "N1",
    "N2", "N3", "A0", "A1", "RS0", "A2", "RS1", "A3", "RS2", "RS3", "K0", "K1", "K2", "K3",
    "E0", "E1", "E2", "E3",
]


def mm(a, b, ca, cb):
    return lax.dot_general(a, b, (((ca,), (cb,)), ((), ())), preferred_element_type=F32)


def kernel(n, heads, dh, groups, scale, q_hbm, k_hbm, v_hbm, w_hbm, y_hbm,
           att_hbm, qg_hbm, kg_hbm, vg_hbm, fg_ref,
           q_ref, k_ref, v_ref, y_ref, att_ref, qg_ref, kg_ref, vg_ref, fq_s, fk_s, gb_s, g_s,
           num_s, gfk_s, vgl_s, a_s, w_ref, p_late, s_late, wt_s, u_first, r_last,
           u_tot, p_chip, r_tot, s_chip, u_recv, p_send, r_recv, s_send,
           f_tot, f_pair, f_recv,
           load_sems, give_sems, take_sems, out_sems, out_give_sems, out_take_sems,
           chip_send_sems, chip_recv_sems, f_pair_sems):
    me = lax.axis_index("seq")
    chips = n // 2
    chip, core = me // 2, lax.rem(me, 2)
    other = 1 - core
    rows = heads * dh // n
    held = heads // 2
    owners, first_owner = chips // 2, chips // 4
    is_owner = (chip >= first_owner) & (chip < first_owner + owners)
    place = chip - first_owner
    tokens = q_hbm.shape[0]
    piece = p_chip.shape[2]
    per_head = dh // piece
    shares = dh // rows
    members = [list(range(g, held, groups)) for g in range(groups)]
    short = chips <= 8
    blocks = [pl.ds(0, tokens), pl.ds(tokens, tokens)]
    ours = pl.ds(pl.multiple_of(core * tokens, tokens), tokens)
    theirs = pl.ds(pl.multiple_of(other * tokens, tokens), tokens)

    def col(j):
        return pl.ds(j * dh, dh)

    def wide(j, parity):
        return pl.ds(pl.multiple_of((2 * j + parity) * dh, dh), dh)

    inputs = ((k_hbm, k_ref), (v_hbm, v_ref), (q_hbm, q_ref), (y_hbm, y_ref))

    def load(a, j):
        src, dst = inputs[a]
        return pltpu.make_async_copy(src.at[:, wide(j, core)], dst.at[ours, col(j)], load_sems.at[a, j])

    def load_map(j):
        return pltpu.make_async_copy(w_hbm.at[2 * j + core], w_ref.at[j], load_sems.at[4, j])

    def to_pair(src, dst, send_sem, recv_sem):
        return pltpu.make_async_remote_copy(
            src_ref=src, dst_ref=dst, send_sem=send_sem, recv_sem=recv_sem,
            device_id={"seq": 2 * chip + other}, device_id_type=MESH)

    def give(a, j):
        src, dst = inputs[a]
        return to_pair(src.at[:, wide(j, other)], dst.at[ours, col(j)], give_sems.at[a], take_sems.at[a, j])

    def ready(a, g):
        for j in members[g]:
            load(a, j).wait()
            give(a, j).wait_recv()

    results = ((att_ref, att_hbm), (qg_ref, qg_hbm), (kg_ref, kg_hbm), (vg_ref, vg_hbm))

    def store(which, j):
        src, dst = results[which]
        return pltpu.make_async_copy(src.at[ours, col(j)], dst.at[:, wide(j, core)], out_sems.at[which, j])

    def give_out(which, j):
        src, dst = results[which]
        return to_pair(src.at[theirs, col(j)], dst.at[:, wide(j, core)], out_give_sems.at[which], out_take_sems.at[which])

    def put_out(which, g):
        for j in members[g]:
            store(which, j).start()
            give_out(which, j).start()

    barrier = pltpu.get_barrier_semaphore()
    pl.semaphore_signal(barrier, inc=1, device_id={"seq": 2 * chip + other}, device_id_type=MESH)

    @pl.when(is_owner)
    def _():
        @pl.loop(1, chips)
        def _(i):
            to = 2 * lax.rem(chip + i, chips) + core
            pl.semaphore_signal(barrier, inc=1, device_id={"seq": to}, device_id_type=MESH)

    for g in range(groups):
        for j in members[g]:
            load_map(j).start()
            load(0, j).start()
            load(1, j).start()
    for j in range(held):
        load(2, j).start()
        load(3, j).start()

    causal = (lax.broadcasted_iota(jnp.int32, (tokens, tokens), 0)
              >= lax.broadcasted_iota(jnp.int32, (tokens, tokens), 1))

    def to_chip(phase, g, src, dst, c):
        return pltpu.make_async_remote_copy(
            src_ref=src, dst_ref=dst, send_sem=chip_send_sems.at[phase],
            recv_sem=chip_recv_sems.at[phase, g], device_id={"seq": 2 * c + core}, device_id_type=MESH)

    def some_chip():
        return lax.rem(chip + 1, chips)

    def to_owners(phase, g, tot, recv):
        @pl.loop(0, owners, unroll=short)
        def _(i):
            at = lax.rem(chip + i, owners)
            c = first_owner + at

            @pl.when(c != chip)
            def _():
                to_chip(phase, g, tot.at[g, at], recv.at[g, chip], c).start()

            @pl.when(c == chip)
            def _():
                recv[g, chip] = tot[g, at]

    def scan(phase, g, recv, send, landing, order):
        @pl.when(is_owner)
        def _():
            sent = recv.at[g, pl.ds(0, chips - 1)]
            to_chip(phase, g, sent, sent, some_chip()).wait_recv()

            def step(i, acc):
                c = order(i)
                send[g, c] = acc.astype(BF16)
                return acc + recv[g, c].astype(F32)

            lax.fori_loop(0, chips, step, jnp.zeros((piece, dh), F32), unroll=short)

            @pl.loop(1, chips, unroll=short)
            def _(i):
                c = lax.rem(chip + i, chips)
                to_chip(phase + 1, g, send.at[g, c], landing.at[g, place], c).start()

            landing[g, place] = send[g, chip]

    def arrive(phase, g, landing):
        @pl.when(is_owner)
        def _():
            sent = landing.at[g, pl.ds(0, owners - 1)]
            to_chip(phase, g, sent, sent, some_chip()).wait_recv()

        @pl.when(jnp.logical_not(is_owner))
        def _():
            to_chip(phase, g, landing.at[g], landing.at[g], some_chip()).wait_recv()

    def put_head(buf, g, k, value):
        buf[g, k * per_head:(k + 1) * per_head] = value.astype(BF16).reshape(per_head, piece, dh)

    def get_head(buf, g, k):
        return buf[g, k * per_head:(k + 1) * per_head].reshape(dh, dh)

    def features(lifted):
        return jnp.where(lifted > 0, lifted + 1.0, jnp.exp(jnp.minimum(lifted, 0.0))).astype(BF16)

    def slope_of(feat):
        return jnp.minimum(feat.astype(F32), 1.0)

    def units(g):
        return [(k, j, b) for k, j in enumerate(members[g]) for b in range(2)]

    def state(g):
        js = members[g]
        lifted = [mm(k_ref[:, col(j)], w_ref[j], 1, 0) for j in js]
        feats = [features(x) for x in lifted]
        sums = [[mm(f[b * tokens:(b + 1) * tokens], v_ref[blocks[b], col(j)], 0, 0) for b in range(2)]
                for j, f in zip(js, feats)]
        for k, j in enumerate(js):
            put_head(u_tot, g, k, sums[k][0] + sums[k][1])
            u_first[j] = sums[k][0]
            fk_s[:, col(j)] = feats[k]

    def local_part(g):
        js = members[g]
        lifted = [mm(q_ref[:, col(j)], w_ref[j], 1, 0) for j in js]
        feats = [features(x) for x in lifted]
        scores = [mm(feats[k][b * tokens:(b + 1) * tokens], fk_s[blocks[b], col(j)], 1, 1) for k, j, b in units(g)]
        scores = [jnp.where(causal, x, 0.0).astype(BF16) for x in scores]
        nums = [mm(x, v_ref[blocks[b], col(j)], 1, 0) for (k, j, b), x in zip(units(g), scores)]
        for k, j in enumerate(js):
            fq_s[:, col(j)] = feats[k]
        for (k, j, b), x, a in zip(units(g), nums, scores):
            a_s[2 * j + b] = a
            num_s[blocks[b], col(j)] = x

    def numerators(g):
        for k, j in enumerate(members[g]):
            p_late[j] = (get_head(p_chip, g, k).astype(F32) + u_first[j]).astype(BF16)
        prefixes = [p_late[j] if b else get_head(p_chip, g, k) for k, j, b in units(g)]
        fqs = [fq_s[blocks[b], col(j)] for k, j, b in units(g)]
        nums = [num_s[blocks[b], col(j)] + mm(f, p, 1, 0) for (k, j, b), f, p in zip(units(g), fqs, prefixes)]
        recips = [lax.rsqrt(jnp.mean(x * x, axis=-1, keepdims=True) + 1e-06) for x in nums]
        ys = [y_ref[blocks[b], col(j)].astype(F32) for k, j, b in units(g)]
        inners = [jnp.mean(y * x, axis=-1, keepdims=True) for y, x in zip(ys, nums)]
        grads = [(r * (y - x * (r * r * m))).astype(BF16) for r, y, x, m in zip(recips, ys, nums, inners)]
        sums = [mm(f, x, 0, 0) for f, x in zip(fqs, grads)]
        for k, j in enumerate(members[g]):
            put_head(r_tot, g, k, sums[2 * k] + sums[2 * k + 1])
            r_last[j] = sums[2 * k + 1]
        for (k, j, b), x, r, gr in zip(units(g), nums, recips, grads):
            att_ref[blocks[b], col(j)] = (x * r).astype(BF16)
            g_s[blocks[b], col(j)] = gr

    def adjoint_part(g):
        us = units(g)
        grads = [g_s[blocks[b], col(j)] for k, j, b in us]
        prefixes = [p_late[j] if b else get_head(p_chip, g, k) for k, j, b in us]
        backs = [mm(x, v_ref[blocks[b], col(j)], 1, 1) for x, (k, j, b) in zip(grads, us)]
        backs = [jnp.where(causal, x, 0.0).astype(BF16) for x in backs]
        gfqs = [mm(s, fk_s[blocks[b], col(j)], 1, 0) + mm(x, p, 1, 1)
                for s, (k, j, b), x, p in zip(backs, us, grads, prefixes)]
        fqs = [fq_s[blocks[b], col(j)] for k, j, b in us]
        gas = [(x * slope_of(f)).astype(BF16) for x, f in zip(gfqs, fqs)]
        qgs = [mm(x, w_ref[j], 1, 1).astype(BF16) for x, (k, j, b) in zip(gas, us)]
        wts = [mm(q_ref[blocks[b], col(j)], x, 0, 0) for x, (k, j, b) in zip(gas, us)]
        gfks = [mm(s, f, 0, 0) for s, f in zip(backs, fqs)]
        vgls = [mm(a_s[2 * j + b], x, 0, 0) for x, (k, j, b) in zip(grads, us)]
        for i, (k, j, b) in enumerate(us):
            qg_ref[blocks[b], col(j)] = qgs[i]
            gfk_s[blocks[b], col(j)] = gfks[i]
            vgl_s[blocks[b], col(j)] = vgls[i]
        for k, j in enumerate(members[g]):
            wt_s[j] = wts[2 * k] + wts[2 * k + 1]

    def key_part(g):
        for k, j in enumerate(members[g]):
            s_late[j] = (get_head(s_chip, g, k).astype(F32) + r_last[j]).astype(BF16)
        us = units(g)
        suffixes = [get_head(s_chip, g, k) if b else s_late[j] for k, j, b in us]
        gfks = [gfk_s[blocks[b], col(j)] + mm(v_ref[blocks[b], col(j)], s, 1, 1) for (k, j, b), s in zip(us, suffixes)]
        gbs = [(x * slope_of(fk_s[blocks[b], col(j)])).astype(BF16) for x, (k, j, b) in zip(gfks, us)]
        wts = [mm(k_ref[blocks[b], col(j)], x, 0, 0) for (k, j, b), x in zip(us, gbs)]
        for (k, j, b), x in zip(us, gbs):
            gb_s[blocks[b], col(j)] = x
        for k, j in enumerate(members[g]):
            whole = (wt_s[j] + (wts[2 * k] + wts[2 * k + 1])).astype(BF16)
            if shares == 1:
                f_tot[0, j] = whole
            else:
                for b in range(shares):
                    f_tot[b % 2, j * (shares // 2) + b // 2] = whole[b * rows:(b + 1) * rows]

    def send_rows(src, c):
        @pl.when(c != chip)
        def _():
            to_chip(4, 0, src, f_recv.at[chip], c).start()

        @pl.when(c == chip)
        def _():
            f_recv[chip] = src[...]

    def swap():
        return to_pair(f_tot.at[other], f_pair, f_pair_sems.at[0], f_pair_sems.at[1])

    def send_weights(g):
        if shares == 1:
            for j in members[g]:
                send_rows(f_tot.at[0, j], j)
        elif g == groups - 1:
            swap().start()
            swap().wait_recv()

            @pl.loop(0, held)
            def _(j):
                @pl.loop(0, shares // 2)
                def _(r):
                    at = j * (shares // 2) + r
                    send_rows(f_tot.at[core, at], (2 * j + core) * (shares // 2) + r)
                    send_rows(f_pair.at[at], (2 * j + other) * (shares // 2) + r)

    def last_part(g):
        us = units(g)
        suffixes = [get_head(s_chip, g, k) if b else s_late[j] for k, j, b in us]
        vgs = [vgl_s[blocks[b], col(j)] + mm(fk_s[blocks[b], col(j)], s, 1, 0) for (k, j, b), s in zip(us, suffixes)]
        kgs = [mm(gb_s[:, col(j)], w_ref[j], 1, 1) for j in members[g]]
        for (k, j, b), x in zip(us, vgs):
            vg_ref[blocks[b], col(j)] = x.astype(BF16)
        for k, j in enumerate(members[g]):
            kg_ref[:, col(j)] = kgs[k].astype(BF16)

    class Steps:
        def U(g):
            if g == 0:
                pl.semaphore_wait(barrier, jnp.where(is_owner, owners, owners + 1))
                for i in range(groups):
                    for j in members[i]:
                        give(0, j).start()
                        give(1, j).start()
            for j in members[g]:
                load_map(j).wait()
            ready(0, g)
            ready(1, g)
            state(g)
            to_owners(0, g, u_tot, u_recv)
            if g == 0:
                for j in range(held):
                    give(2, j).start()
            if g == groups - 1:
                for j in range(held):
                    give(3, j).start()

        def L(g):
            ready(2, g)
            local_part(g)

        def S(g):
            scan(0, g, u_recv, p_send, p_chip, lambda i: i)

        def N(g):
            ready(3, g)
            arrive(1, g, p_chip)
            numerators(g)
            to_owners(2, g, r_tot, r_recv)
            put_out(0, g)

        def A(g):
            adjoint_part(g)
            put_out(1, g)

        def RS(g):
            scan(2, g, r_recv, s_send, s_chip, lambda i: chips - 1 - i)

        def K(g):
            arrive(3, g, s_chip)
            key_part(g)
            send_weights(g)

        def E(g):
            last_part(g)
            put_out(2, g)
            put_out(3, g)

    for step in ORDER:
        name, g = step[:-1], int(step[-1])
        if g < groups:
            getattr(Steps, name)(g)

    some = f_recv.at[pl.ds(0, chips - 1)]
    to_chip(4, 0, some, some, some_chip()).wait_recv()

    def collect(c, acc):
        return acc + f_recv[c].astype(F32)

    fg_ref[...] = lax.fori_loop(0, chips, collect, jnp.zeros((rows, dh), F32), unroll=short) * scale

    for which in range(4):
        for j in range(held):
            store(which, j).wait()
        block = results[which][0].at[pl.ds(0, tokens)]
        both = to_pair(block, block, out_give_sems.at[which], out_take_sems.at[which])
        both.wait_send()
        both.wait_recv()
        to_pair(block, block, give_sems.at[which], out_take_sems.at[which]).wait_send()

    @pl.when(is_owner)
    def _():
        for phase, tot, send in ((0, u_tot, p_send), (2, r_tot, s_send)):
            sent = tot.at[:, pl.ds(0, owners - 1)]
            to_chip(phase, 0, sent, sent, some_chip()).wait_send()
            sent = send.at[:, pl.ds(0, chips - 1)]
            to_chip(phase + 1, 0, sent, sent, some_chip()).wait_send()

    @pl.when(jnp.logical_not(is_owner))
    def _():
        for phase, tot in ((0, u_tot), (2, r_tot)):
            to_chip(phase, 0, tot, tot, some_chip()).wait_send()

    to_chip(4, 0, some, some, some_chip()).wait_send()
    if shares > 1:
        swap().wait_send()


def copy_out(*refs):
    writes = [pltpu.make_async_copy(refs[i], refs[5 + i], refs[10].at[i]) for i in range(5)]
    for write in writes:
        write.start()
    for write in writes:
        write.wait()


def local(queries, keys, values, feature_map, out_grad):
    tokens, width = queries.shape
    heads, dh, _ = feature_map.shape
    n = lax.axis_size("seq")
    chips, rows, held = n // 2, heads * dh // n, heads // 2
    owners = chips // 2
    groups = max(1, min(GROUPS, held * dh // (owners * 16)))
    piece = held // groups * dh // owners
    slots = held * max(2, dh // rows) // 2
    wide = jax.ShapeDtypeStruct((tokens, width), BF16)
    vmem = pl.BlockSpec(memory_space=pltpu.VMEM)
    hbm = pl.BlockSpec(memory_space=pltpu.HBM)
    shapes = (wide, wide, wide, wide, jax.ShapeDtypeStruct((rows, dh), F32))
    outs = pl.pallas_call(
        functools.partial(kernel, n, heads, dh, groups, 1.0 / math.sqrt(tokens * n)),
        out_shape=(wide, pltpu.VMEM(wide.shape, BF16), pltpu.VMEM(wide.shape, BF16), pltpu.VMEM(wide.shape, BF16), shapes[4]),
        in_specs=[hbm] * 5,
        out_specs=(hbm, vmem, vmem, vmem, vmem),
        scratch_shapes=[pltpu.VMEM((2 * tokens, width // 2), BF16)] * 12 + [
            pltpu.VMEM((2 * tokens, width // 2), F32)] * 3 + [
            pltpu.VMEM((heads, tokens, tokens), BF16)] + [
            pltpu.VMEM((held, dh, dh), BF16)] * 3 + [
            pltpu.VMEM((held, dh, dh), F32)] * 3 + [
            pltpu.VMEM((groups, owners, piece, dh), BF16)] * 4 + [
            pltpu.VMEM((groups, chips, piece, dh), BF16)] * 4 + [
            pltpu.VMEM((2, slots, rows, dh), BF16),
            pltpu.VMEM((slots, rows, dh), BF16),
            pltpu.VMEM((chips, rows, dh), BF16),
            pltpu.SemaphoreType.DMA((5, held)),
            pltpu.SemaphoreType.DMA((4,)),
            pltpu.SemaphoreType.DMA((4, held)),
            pltpu.SemaphoreType.DMA((4, held)),
            pltpu.SemaphoreType.DMA((4,)),
            pltpu.SemaphoreType.DMA((4,)),
            pltpu.SemaphoreType.DMA((5,)),
            pltpu.SemaphoreType.DMA((5, groups)),
            pltpu.SemaphoreType.DMA((2,)),
        ],
        compiler_params=pltpu.CompilerParams(
            collective_id=0, has_side_effects=True, vmem_limit_bytes=40 << 20),
        name="linear_attention",
    )(*[pltpu.with_memory_space_constraint(x, pltpu.HBM) for x in (queries, keys, values, feature_map, out_grad)])
    outs = [pltpu.with_memory_space_constraint(x, pltpu.VMEM) if i in DIRECT else x for i, x in enumerate(outs)]
    outs = pl.pallas_call(
        copy_out,
        out_shape=shapes,
        in_specs=[vmem if i in DIRECT else pl.BlockSpec(memory_space=pl.ANY) for i in range(5)],
        out_specs=(hbm,) * 5,
        scratch_shapes=[pltpu.SemaphoreType.DMA((5,))],
        compiler_params=pltpu.CompilerParams(vmem_limit_bytes=16 << 20),
        name="copy_out",
    )(*outs)
    return tuple(outs[:4]) + (outs[4].reshape(rows * dh),)


def solution(mesh):
    wide = P(("grp", "seq"), None)
    return jax.shard_map(
        local, mesh=mesh, in_specs=(wide, wide, wide, P(), wide),
        out_specs=(wide, wide, wide, wide, P(("grp", "seq"))), check_vma=False)
```

```python
import functools
import math

import jax
import jax.numpy as jnp
from jax import lax
from jax.experimental import pallas as pl
from jax.experimental.pallas import tpu as pltpu
from jax.sharding import PartitionSpec as P

MESH = pl.DeviceIdType.MESH
BF16 = jnp.bfloat16
F32 = jnp.float32
GROUPS = 4
DIRECT = (2, 3, 1,)
ORDER = [
    "U0", "U1", "U2", "U3", "L0", "L1", "S0", "L2", "S1", "L3", "S2", "S3", "N0", "N1",
    "N2", "N3", "A0", "A1", "RS0", "A2", "RS1", "A3", "RS2", "RS3", "K0", "K1", "K2", "K3",
    "E0", "E1", "E2", "E3",
]


def mm(a, b, ca, cb):
    return lax.dot_general(a, b, (((ca,), (cb,)), ((), ())), preferred_element_type=F32)


def kernel(n, heads, dh, groups, scale, q_hbm, k_hbm, v_hbm, w_hbm, y_hbm,
           att_hbm, qg_hbm, kg_hbm, vg_hbm, fg_ref,
           q_ref, k_ref, v_ref, y_ref, att_ref, qg_ref, kg_ref, vg_ref, fq_s, fk_s, gb_s, g_s,
           num_s, gfk_s, vgl_s, a_s, w_ref, p_late, s_late, wt_s, u_first, r_last,
           u_tot, p_chip, r_tot, s_chip, u_recv, p_send, r_recv, s_send,
           f_tot, f_pair, f_recv,
           load_sems, give_sems, take_sems, out_sems, out_give_sems, out_take_sems,
           chip_send_sems, chip_recv_sems, f_pair_sems):
    me = lax.axis_index("seq")
    chips = n // 2
    chip, core = me // 2, lax.rem(me, 2)
    other = 1 - core
    rows = heads * dh // n
    held = heads // 2
    owners, first_owner = chips // 2, chips // 4
    is_owner = (chip >= first_owner) & (chip < first_owner + owners)
    place = chip - first_owner
    side = chip // (chips // 2)
    tokens = q_hbm.shape[0]
    piece = p_chip.shape[2]
    per_head = dh // piece
    shares = dh // rows
    members = [list(range(g, held, groups)) for g in range(groups)]
    short = chips <= 8
    blocks = [pl.ds(0, tokens), pl.ds(tokens, tokens)]
    ours = pl.ds(pl.multiple_of(core * tokens, tokens), tokens)
    theirs = pl.ds(pl.multiple_of(other * tokens, tokens), tokens)

    def col(j):
        return pl.ds(j * dh, dh)

    def wide(j, parity):
        return pl.ds(pl.multiple_of((2 * j + parity) * dh, dh), dh)

    inputs = ((k_hbm, k_ref), (v_hbm, v_ref), (q_hbm, q_ref), (y_hbm, y_ref))

    def load(a, j):
        src, dst = inputs[a]
        return pltpu.make_async_copy(src.at[:, wide(j, core)], dst.at[ours, col(j)], load_sems.at[a, j])

    def load_map(j):
        return pltpu.make_async_copy(w_hbm.at[2 * j + core], w_ref.at[j], load_sems.at[4, j])

    def to_pair(src, dst, send_sem, recv_sem):
        return pltpu.make_async_remote_copy(
            src_ref=src, dst_ref=dst, send_sem=send_sem, recv_sem=recv_sem,
            device_id={"seq": 2 * chip + other}, device_id_type=MESH)

    def give(a, j):
        src, dst = inputs[a]
        return to_pair(src.at[:, wide(j, other)], dst.at[ours, col(j)], give_sems.at[a], take_sems.at[a, j])

    def ready(a, g):
        for j in members[g]:
            load(a, j).wait()
            give(a, j).wait_recv()

    results = ((att_ref, att_hbm), (qg_ref, qg_hbm), (kg_ref, kg_hbm), (vg_ref, vg_hbm))

    def store(which, j):
        src, dst = results[which]
        return pltpu.make_async_copy(src.at[ours, col(j)], dst.at[:, wide(j, core)], out_sems.at[which, j])

    def give_out(which, j):
        src, dst = results[which]
        return to_pair(src.at[theirs, col(j)], dst.at[:, wide(j, core)], out_give_sems.at[which], out_take_sems.at[which])

    def put_out(which, g):
        for j in members[g]:
            store(which, j).start()
            give_out(which, j).start()

    barrier = pltpu.get_barrier_semaphore()
    pl.semaphore_signal(barrier, inc=1, device_id={"seq": 2 * chip + other}, device_id_type=MESH)

    @pl.when(is_owner)
    def _():
        @pl.loop(1, chips)
        def _(i):
            to = 2 * lax.rem(chip + i, chips) + core
            pl.semaphore_signal(barrier, inc=1, device_id={"seq": to}, device_id_type=MESH)

    for g in range(groups):
        for j in members[g]:
            load_map(j).start()
            load(0, j).start()
            load(1, j).start()
    for j in range(held):
        load(2, j).start()
        load(3, j).start()

    causal = (lax.broadcasted_iota(jnp.int32, (tokens, tokens), 0)
              >= lax.broadcasted_iota(jnp.int32, (tokens, tokens), 1))

    def to_chip(phase, g, src, dst, c):
        return pltpu.make_async_remote_copy(
            src_ref=src, dst_ref=dst, send_sem=chip_send_sems.at[phase],
            recv_sem=chip_recv_sems.at[phase, g], device_id={"seq": 2 * c + core}, device_id_type=MESH)

    def some_chip():
        return lax.rem(chip + 1, chips)

    def to_owners(phase, g, tot, recv):
        @pl.loop(0, owners, unroll=short)
        def _(i):
            at = lax.rem(side * (owners // 2) + i, owners)
            c = first_owner + at

            @pl.when(c != chip)
            def _():
                to_chip(phase, g, tot.at[g, at], recv.at[g, chip], c).start()

            @pl.when(c == chip)
            def _():
                recv[g, chip] = tot[g, at]

    def scan(phase, g, recv, send, landing, order):
        @pl.when(is_owner)
        def _():
            sent = recv.at[g, pl.ds(0, chips - 1)]
            to_chip(phase, g, sent, sent, some_chip()).wait_recv()

            def step(i, acc):
                c = order(i)
                send[g, c] = acc.astype(BF16)
                return acc + recv[g, c].astype(F32)

            lax.fori_loop(0, chips, step, jnp.zeros((piece, dh), F32), unroll=short)

            @pl.loop(1, chips, unroll=short)
            def _(i):
                c = lax.rem(chip + i, chips)
                to_chip(phase + 1, g, send.at[g, c], landing.at[g, place], c).start()

            landing[g, place] = send[g, chip]

    def arrive(phase, g, landing):
        @pl.when(is_owner)
        def _():
            sent = landing.at[g, pl.ds(0, owners - 1)]
            to_chip(phase, g, sent, sent, some_chip()).wait_recv()

        @pl.when(jnp.logical_not(is_owner))
        def _():
            to_chip(phase, g, landing.at[g], landing.at[g], some_chip()).wait_recv()

    def put_head(buf, g, k, value):
        buf[g, k * per_head:(k + 1) * per_head] = value.astype(BF16).reshape(per_head, piece, dh)

    def get_head(buf, g, k):
        return buf[g, k * per_head:(k + 1) * per_head].reshape(dh, dh)

    def features(lifted):
        return jnp.where(lifted > 0, lifted + 1.0, jnp.exp(jnp.minimum(lifted, 0.0))).astype(BF16)

    def slope_of(feat):
        return jnp.minimum(feat.astype(F32), 1.0)

    def units(g):
        return [(k, j, b) for k, j in enumerate(members[g]) for b in range(2)]

    def state(g):
        js = members[g]
        lifted = [mm(k_ref[:, col(j)], w_ref[j], 1, 0) for j in js]
        feats = [features(x) for x in lifted]
        sums = [[mm(f[b * tokens:(b + 1) * tokens], v_ref[blocks[b], col(j)], 0, 0) for b in range(2)]
                for j, f in zip(js, feats)]
        for k, j in enumerate(js):
            put_head(u_tot, g, k, sums[k][0] + sums[k][1])
            u_first[j] = sums[k][0]
            fk_s[:, col(j)] = feats[k]

    def local_part(g):
        js = members[g]
        lifted = [mm(q_ref[:, col(j)], w_ref[j], 1, 0) for j in js]
        feats = [features(x) for x in lifted]
        scores = [mm(feats[k][b * tokens:(b + 1) * tokens], fk_s[blocks[b], col(j)], 1, 1) for k, j, b in units(g)]
        scores = [jnp.where(causal, x, 0.0).astype(BF16) for x in scores]
        nums = [mm(x, v_ref[blocks[b], col(j)], 1, 0) for (k, j, b), x in zip(units(g), scores)]
        for k, j in enumerate(js):
            fq_s[:, col(j)] = feats[k]
        for (k, j, b), x, a in zip(units(g), nums, scores):
            a_s[2 * j + b] = a
            num_s[blocks[b], col(j)] = x

    def numerators(g):
        for k, j in enumerate(members[g]):
            p_late[j] = (get_head(p_chip, g, k).astype(F32) + u_first[j]).astype(BF16)
        prefixes = [p_late[j] if b else get_head(p_chip, g, k) for k, j, b in units(g)]
        fqs = [fq_s[blocks[b], col(j)] for k, j, b in units(g)]
        nums = [num_s[blocks[b], col(j)] + mm(f, p, 1, 0) for (k, j, b), f, p in zip(units(g), fqs, prefixes)]
        recips = [lax.rsqrt(jnp.mean(x * x, axis=-1, keepdims=True) + 1e-06) for x in nums]
        ys = [y_ref[blocks[b], col(j)].astype(F32) for k, j, b in units(g)]
        inners = [jnp.mean(y * x, axis=-1, keepdims=True) for y, x in zip(ys, nums)]
        grads = [(r * (y - x * (r * r * m))).astype(BF16) for r, y, x, m in zip(recips, ys, nums, inners)]
        sums = [mm(f, x, 0, 0) for f, x in zip(fqs, grads)]
        for k, j in enumerate(members[g]):
            put_head(r_tot, g, k, sums[2 * k] + sums[2 * k + 1])
            r_last[j] = sums[2 * k + 1]
        for (k, j, b), x, r, gr in zip(units(g), nums, recips, grads):
            att_ref[blocks[b], col(j)] = (x * r).astype(BF16)
            g_s[blocks[b], col(j)] = gr

    def adjoint_part(g):
        us = units(g)
        grads = [g_s[blocks[b], col(j)] for k, j, b in us]
        prefixes = [p_late[j] if b else get_head(p_chip, g, k) for k, j, b in us]
        backs = [mm(x, v_ref[blocks[b], col(j)], 1, 1) for x, (k, j, b) in zip(grads, us)]
        backs = [jnp.where(causal, x, 0.0).astype(BF16) for x in backs]
        gfqs = [mm(s, fk_s[blocks[b], col(j)], 1, 0) + mm(x, p, 1, 1)
                for s, (k, j, b), x, p in zip(backs, us, grads, prefixes)]
        fqs = [fq_s[blocks[b], col(j)] for k, j, b in us]
        gas = [(x * slope_of(f)).astype(BF16) for x, f in zip(gfqs, fqs)]
        qgs = [mm(x, w_ref[j], 1, 1).astype(BF16) for x, (k, j, b) in zip(gas, us)]
        wts = [mm(q_ref[blocks[b], col(j)], x, 0, 0) for x, (k, j, b) in zip(gas, us)]
        gfks = [mm(s, f, 0, 0) for s, f in zip(backs, fqs)]
        vgls = [mm(a_s[2 * j + b], x, 0, 0) for x, (k, j, b) in zip(grads, us)]
        for i, (k, j, b) in enumerate(us):
            qg_ref[blocks[b], col(j)] = qgs[i]
            gfk_s[blocks[b], col(j)] = gfks[i]
            vgl_s[blocks[b], col(j)] = vgls[i]
        for k, j in enumerate(members[g]):
            wt_s[j] = wts[2 * k] + wts[2 * k + 1]

    def key_part(g):
        for k, j in enumerate(members[g]):
            s_late[j] = (get_head(s_chip, g, k).astype(F32) + r_last[j]).astype(BF16)
        us = units(g)
        suffixes = [get_head(s_chip, g, k) if b else s_late[j] for k, j, b in us]
        gfks = [gfk_s[blocks[b], col(j)] + mm(v_ref[blocks[b], col(j)], s, 1, 1) for (k, j, b), s in zip(us, suffixes)]
        gbs = [(x * slope_of(fk_s[blocks[b], col(j)])).astype(BF16) for x, (k, j, b) in zip(gfks, us)]
        wts = [mm(k_ref[blocks[b], col(j)], x, 0, 0) for (k, j, b), x in zip(us, gbs)]
        for (k, j, b), x in zip(us, gbs):
            gb_s[blocks[b], col(j)] = x
        for k, j in enumerate(members[g]):
            whole = (wt_s[j] + (wts[2 * k] + wts[2 * k + 1])).astype(BF16)
            if shares == 1:
                f_tot[0, j] = whole
            else:
                for b in range(shares):
                    f_tot[b % 2, j * (shares // 2) + b // 2] = whole[b * rows:(b + 1) * rows]

    def send_rows(src, c):
        @pl.when(c != chip)
        def _():
            to_chip(4, 0, src, f_recv.at[chip], c).start()

        @pl.when(c == chip)
        def _():
            f_recv[chip] = src[...]

    def swap():
        return to_pair(f_tot.at[other], f_pair, f_pair_sems.at[0], f_pair_sems.at[1])

    def send_weights(g):
        if shares == 1:
            for j in members[g]:
                send_rows(f_tot.at[0, j], j)
        elif g == groups - 1:
            swap().start()
            swap().wait_recv()

            @pl.loop(0, held)
            def _(j):
                @pl.loop(0, shares // 2)
                def _(r):
                    at = j * (shares // 2) + r
                    send_rows(f_tot.at[core, at], (2 * j + core) * (shares // 2) + r)
                    send_rows(f_pair.at[at], (2 * j + other) * (shares // 2) + r)

    def last_part(g):
        us = units(g)
        suffixes = [get_head(s_chip, g, k) if b else s_late[j] for k, j, b in us]
        vgs = [vgl_s[blocks[b], col(j)] + mm(fk_s[blocks[b], col(j)], s, 1, 0) for (k, j, b), s in zip(us, suffixes)]
        kgs = [mm(gb_s[:, col(j)], w_ref[j], 1, 1) for j in members[g]]
        for (k, j, b), x in zip(us, vgs):
            vg_ref[blocks[b], col(j)] = x.astype(BF16)
        for k, j in enumerate(members[g]):
            kg_ref[:, col(j)] = kgs[k].astype(BF16)

    class Steps:
        def U(g):
            if g == 0:
                pl.semaphore_wait(barrier, jnp.where(is_owner, owners, owners + 1))
                for i in range(groups):
                    for j in members[i]:
                        give(0, j).start()
                        give(1, j).start()
            for j in members[g]:
                load_map(j).wait()
            ready(0, g)
            ready(1, g)
            state(g)
            to_owners(0, g, u_tot, u_recv)
            if g == 0:
                for j in range(held):
                    give(2, j).start()
            if g == groups - 1:
                for j in range(held):
                    give(3, j).start()

        def L(g):
            ready(2, g)
            local_part(g)

        def S(g):
            scan(0, g, u_recv, p_send, p_chip, lambda i: i)

        def N(g):
            ready(3, g)
            arrive(1, g, p_chip)
            numerators(g)
            to_owners(2, g, r_tot, r_recv)
            put_out(0, g)

        def A(g):
            adjoint_part(g)
            put_out(1, g)

        def RS(g):
            scan(2, g, r_recv, s_send, s_chip, lambda i: chips - 1 - i)

        def K(g):
            arrive(3, g, s_chip)
            key_part(g)
            send_weights(g)

        def E(g):
            last_part(g)
            put_out(2, g)
            put_out(3, g)

    for step in ORDER:
        name, g = step[:-1], int(step[-1])
        if g < groups:
            getattr(Steps, name)(g)

    some = f_recv.at[pl.ds(0, chips - 1)]
    to_chip(4, 0, some, some, some_chip()).wait_recv()

    def collect(c, acc):
        return acc + f_recv[c].astype(F32)

    fg_ref[...] = lax.fori_loop(0, chips, collect, jnp.zeros((rows, dh), F32), unroll=short) * scale

    for which in range(4):
        for j in range(held):
            store(which, j).wait()
        block = results[which][0].at[pl.ds(0, tokens)]
        both = to_pair(block, block, out_give_sems.at[which], out_take_sems.at[which])
        both.wait_send()
        both.wait_recv()
        to_pair(block, block, give_sems.at[which], out_take_sems.at[which]).wait_send()

    @pl.when(is_owner)
    def _():
        for phase, tot, send in ((0, u_tot, p_send), (2, r_tot, s_send)):
            sent = tot.at[:, pl.ds(0, owners - 1)]
            to_chip(phase, 0, sent, sent, some_chip()).wait_send()
            sent = send.at[:, pl.ds(0, chips - 1)]
            to_chip(phase + 1, 0, sent, sent, some_chip()).wait_send()

    @pl.when(jnp.logical_not(is_owner))
    def _():
        for phase, tot in ((0, u_tot), (2, r_tot)):
            to_chip(phase, 0, tot, tot, some_chip()).wait_send()

    to_chip(4, 0, some, some, some_chip()).wait_send()
    if shares > 1:
        swap().wait_send()


def copy_out(*refs):
    writes = [pltpu.make_async_copy(refs[i], refs[5 + i], refs[10].at[i]) for i in range(5)]
    for write in writes:
        write.start()
    for write in writes:
        write.wait()


def local(queries, keys, values, feature_map, out_grad):
    tokens, width = queries.shape
    heads, dh, _ = feature_map.shape
    n = lax.axis_size("seq")
    chips, rows, held = n // 2, heads * dh // n, heads // 2
    owners = chips // 2
    groups = max(1, min(GROUPS, held * dh // (owners * 16)))
    piece = held // groups * dh // owners
    slots = held * max(2, dh // rows) // 2
    wide = jax.ShapeDtypeStruct((tokens, width), BF16)
    vmem = pl.BlockSpec(memory_space=pltpu.VMEM)
    hbm = pl.BlockSpec(memory_space=pltpu.HBM)
    shapes = (wide, wide, wide, wide, jax.ShapeDtypeStruct((rows, dh), F32))
    outs = pl.pallas_call(
        functools.partial(kernel, n, heads, dh, groups, 1.0 / math.sqrt(tokens * n)),
        out_shape=(wide, pltpu.VMEM(wide.shape, BF16), pltpu.VMEM(wide.shape, BF16), pltpu.VMEM(wide.shape, BF16), shapes[4]),
        in_specs=[hbm] * 5,
        out_specs=(hbm, vmem, vmem, vmem, vmem),
        scratch_shapes=[pltpu.VMEM((2 * tokens, width // 2), BF16)] * 12 + [
            pltpu.VMEM((2 * tokens, width // 2), F32)] * 3 + [
            pltpu.VMEM((heads, tokens, tokens), BF16)] + [
            pltpu.VMEM((held, dh, dh), BF16)] * 3 + [
            pltpu.VMEM((held, dh, dh), F32)] * 3 + [
            pltpu.VMEM((groups, owners, piece, dh), BF16)] * 4 + [
            pltpu.VMEM((groups, chips, piece, dh), BF16)] * 4 + [
            pltpu.VMEM((2, slots, rows, dh), BF16),
            pltpu.VMEM((slots, rows, dh), BF16),
            pltpu.VMEM((chips, rows, dh), BF16),
            pltpu.SemaphoreType.DMA((5, held)),
            pltpu.SemaphoreType.DMA((4,)),
            pltpu.SemaphoreType.DMA((4, held)),
            pltpu.SemaphoreType.DMA((4, held)),
            pltpu.SemaphoreType.DMA((4,)),
            pltpu.SemaphoreType.DMA((4,)),
            pltpu.SemaphoreType.DMA((5,)),
            pltpu.SemaphoreType.DMA((5, groups)),
            pltpu.SemaphoreType.DMA((2,)),
        ],
        compiler_params=pltpu.CompilerParams(
            collective_id=0, has_side_effects=True, vmem_limit_bytes=40 << 20),
        name="linear_attention",
    )(*[pltpu.with_memory_space_constraint(x, pltpu.HBM) for x in (queries, keys, values, feature_map, out_grad)])
    outs = [pltpu.with_memory_space_constraint(x, pltpu.VMEM) if i in DIRECT else x for i, x in enumerate(outs)]
    outs = pl.pallas_call(
        copy_out,
        out_shape=shapes,
        in_specs=[vmem if i in DIRECT else pl.BlockSpec(memory_space=pl.ANY) for i in range(5)],
        out_specs=(hbm,) * 5,
        scratch_shapes=[pltpu.SemaphoreType.DMA((5,))],
        compiler_params=pltpu.CompilerParams(vmem_limit_bytes=16 << 20),
        name="copy_out",
    )(*outs)
    return tuple(outs[:4]) + (outs[4].reshape(rows * dh),)


def solution(mesh):
    wide = P(("grp", "seq"), None)
    return jax.shard_map(
        local, mesh=mesh, in_specs=(wide, wide, wide, P(), wide),
        out_specs=(wide, wide, wide, wide, P(("grp", "seq"))), check_vma=False)
```

```python
import functools
import math

import jax
import jax.numpy as jnp
from jax import lax
from jax.experimental import pallas as pl
from jax.experimental.pallas import tpu as pltpu
from jax.sharding import PartitionSpec as P

MESH = pl.DeviceIdType.MESH
BF16 = jnp.bfloat16
F32 = jnp.float32
GROUPS = 4
DIRECT = (2, 3, 1,)
ORDER = [
    "U0", "U1", "U2", "U3", "L0", "L1", "S0", "L2", "S1", "L3", "S2", "S3", "N0", "N1",
    "N2", "N3", "A0", "A1", "RS0", "A2", "RS1", "A3", "RS2", "RS3", "K0", "K1", "K2", "K3",
    "E0", "E1", "E2", "E3",
]


def mm(a, b, ca, cb):
    return lax.dot_general(a, b, (((ca,), (cb,)), ((), ())), preferred_element_type=F32)


def kernel(n, heads, dh, groups, scale, q_hbm, k_hbm, v_hbm, w_hbm, y_hbm,
           att_hbm, qg_hbm, kg_hbm, vg_hbm, fg_ref,
           q_ref, k_ref, v_ref, y_ref, att_ref, qg_ref, kg_ref, vg_ref, fq_s, fk_s, gb_s, g_s,
           num_s, gfk_s, vgl_s, a_s, w_ref, p_late, s_late, wt_s, u_first, r_last,
           u_tot, p_chip, r_tot, s_chip, u_recv, p_send, r_recv, s_send,
           f_tot, f_pair, f_recv,
           load_sems, give_sems, take_sems, out_sems, out_give_sems, out_take_sems,
           chip_send_sems, chip_recv_sems, f_pair_sems):
    me = lax.axis_index("seq")
    chips = n // 2
    chip, core = me // 2, lax.rem(me, 2)
    other = 1 - core
    rows = heads * dh // n
    held = heads // 2
    owners, first_owner = chips // 2, chips // 4
    is_owner = (chip >= first_owner) & (chip < first_owner + owners)
    place = chip - first_owner
    side = chip // (chips // 2)
    tokens = q_hbm.shape[0]
    piece = p_chip.shape[2]
    per_head = dh // piece
    shares = dh // rows
    members = [list(range(g, held, groups)) for g in range(groups)]
    short = chips <= 8
    blocks = [pl.ds(0, tokens), pl.ds(tokens, tokens)]
    ours = pl.ds(pl.multiple_of(core * tokens, tokens), tokens)
    theirs = pl.ds(pl.multiple_of(other * tokens, tokens), tokens)

    def col(j):
        return pl.ds(j * dh, dh)

    def wide(j, parity):
        return pl.ds(pl.multiple_of((2 * j + parity) * dh, dh), dh)

    inputs = ((k_hbm, k_ref), (v_hbm, v_ref), (q_hbm, q_ref), (y_hbm, y_ref))

    def load(a, j):
        src, dst = inputs[a]
        return pltpu.make_async_copy(src.at[:, wide(j, core)], dst.at[ours, col(j)], load_sems.at[a, j])

    def load_map(j):
        return pltpu.make_async_copy(w_hbm.at[2 * j + core], w_ref.at[j], load_sems.at[4, j])

    def to_pair(src, dst, send_sem, recv_sem):
        return pltpu.make_async_remote_copy(
            src_ref=src, dst_ref=dst, send_sem=send_sem, recv_sem=recv_sem,
            device_id={"seq": 2 * chip + other}, device_id_type=MESH)

    def give(a, j):
        src, dst = inputs[a]
        return to_pair(src.at[:, wide(j, other)], dst.at[ours, col(j)], give_sems.at[a], take_sems.at[a, j])

    def ready(a, g):
        for j in members[g]:
            load(a, j).wait()
            give(a, j).wait_recv()

    results = ((att_ref, att_hbm), (qg_ref, qg_hbm), (kg_ref, kg_hbm), (vg_ref, vg_hbm))

    def store(which, j):
        src, dst = results[which]
        return pltpu.make_async_copy(src.at[ours, col(j)], dst.at[:, wide(j, core)], out_sems.at[which, j])

    def give_out(which, j):
        src, dst = results[which]
        return to_pair(src.at[theirs, col(j)], dst.at[:, wide(j, core)], out_give_sems.at[which], out_take_sems.at[which])

    def put_out(which, g):
        for j in members[g]:
            store(which, j).start(priority=1)
            give_out(which, j).start()

    barrier = pltpu.get_barrier_semaphore()
    pl.semaphore_signal(barrier, inc=1, device_id={"seq": 2 * chip + other}, device_id_type=MESH)

    @pl.when(is_owner)
    def _():
        @pl.loop(1, chips)
        def _(i):
            to = 2 * lax.rem(chip + i, chips) + core
            pl.semaphore_signal(barrier, inc=1, device_id={"seq": to}, device_id_type=MESH)

    for g in range(groups):
        for j in members[g]:
            load_map(j).start()
            load(0, j).start()
            load(1, j).start()
    for j in range(held):
        load(2, j).start(priority=1)
        load(3, j).start(priority=1)

    causal = (lax.broadcasted_iota(jnp.int32, (tokens, tokens), 0)
              >= lax.broadcasted_iota(jnp.int32, (tokens, tokens), 1))

    def to_chip(phase, g, src, dst, c):
        return pltpu.make_async_remote_copy(
            src_ref=src, dst_ref=dst, send_sem=chip_send_sems.at[phase],
            recv_sem=chip_recv_sems.at[phase, g], device_id={"seq": 2 * c + core}, device_id_type=MESH)

    def some_chip():
        return lax.rem(chip + 1, chips)

    def to_owners(phase, g, tot, recv):
        @pl.loop(0, owners, unroll=short)
        def _(i):
            at = lax.rem(side * (owners // 2) + i, owners)
            c = first_owner + at

            @pl.when(c != chip)
            def _():
                to_chip(phase, g, tot.at[g, at], recv.at[g, chip], c).start()

            @pl.when(c == chip)
            def _():
                recv[g, chip] = tot[g, at]

    def scan(phase, g, recv, send, landing, order):
        @pl.when(is_owner)
        def _():
            sent = recv.at[g, pl.ds(0, chips - 1)]
            to_chip(phase, g, sent, sent, some_chip()).wait_recv()

            def step(i, acc):
                c = order(i)
                send[g, c] = acc.astype(BF16)
                return acc + recv[g, c].astype(F32)

            lax.fori_loop(0, chips, step, jnp.zeros((piece, dh), F32), unroll=short)

            @pl.loop(1, chips, unroll=short)
            def _(i):
                c = lax.rem(chip + i, chips)
                to_chip(phase + 1, g, send.at[g, c], landing.at[g, place], c).start()

            landing[g, place] = send[g, chip]

    def arrive(phase, g, landing):
        @pl.when(is_owner)
        def _():
            sent = landing.at[g, pl.ds(0, owners - 1)]
            to_chip(phase, g, sent, sent, some_chip()).wait_recv()

        @pl.when(jnp.logical_not(is_owner))
        def _():
            to_chip(phase, g, landing.at[g], landing.at[g], some_chip()).wait_recv()

    def put_head(buf, g, k, value):
        buf[g, k * per_head:(k + 1) * per_head] = value.astype(BF16).reshape(per_head, piece, dh)

    def get_head(buf, g, k):
        return buf[g, k * per_head:(k + 1) * per_head].reshape(dh, dh)

    def features(lifted):
        return jnp.where(lifted > 0, lifted + 1.0, jnp.exp(jnp.minimum(lifted, 0.0))).astype(BF16)

    def slope_of(feat):
        return jnp.minimum(feat.astype(F32), 1.0)

    def units(g):
        return [(k, j, b) for k, j in enumerate(members[g]) for b in range(2)]

    def state(g):
        js = members[g]
        lifted = [mm(k_ref[:, col(j)], w_ref[j], 1, 0) for j in js]
        feats = [features(x) for x in lifted]
        sums = [[mm(f[b * tokens:(b + 1) * tokens], v_ref[blocks[b], col(j)], 0, 0) for b in range(2)]
                for j, f in zip(js, feats)]
        for k, j in enumerate(js):
            put_head(u_tot, g, k, sums[k][0] + sums[k][1])
            u_first[j] = sums[k][0]
            fk_s[:, col(j)] = feats[k]

    def local_part(g):
        js = members[g]
        lifted = [mm(q_ref[:, col(j)], w_ref[j], 1, 0) for j in js]
        feats = [features(x) for x in lifted]
        scores = [mm(feats[k][b * tokens:(b + 1) * tokens], fk_s[blocks[b], col(j)], 1, 1) for k, j, b in units(g)]
        scores = [jnp.where(causal, x, 0.0).astype(BF16) for x in scores]
        nums = [mm(x, v_ref[blocks[b], col(j)], 1, 0) for (k, j, b), x in zip(units(g), scores)]
        for k, j in enumerate(js):
            fq_s[:, col(j)] = feats[k]
        for (k, j, b), x, a in zip(units(g), nums, scores):
            a_s[2 * j + b] = a
            num_s[blocks[b], col(j)] = x

    def numerators(g):
        for k, j in enumerate(members[g]):
            p_late[j] = (get_head(p_chip, g, k).astype(F32) + u_first[j]).astype(BF16)
        prefixes = [p_late[j] if b else get_head(p_chip, g, k) for k, j, b in units(g)]
        fqs = [fq_s[blocks[b], col(j)] for k, j, b in units(g)]
        nums = [num_s[blocks[b], col(j)] + mm(f, p, 1, 0) for (k, j, b), f, p in zip(units(g), fqs, prefixes)]
        recips = [lax.rsqrt(jnp.mean(x * x, axis=-1, keepdims=True) + 1e-06) for x in nums]
        ys = [y_ref[blocks[b], col(j)].astype(F32) for k, j, b in units(g)]
        inners = [jnp.mean(y * x, axis=-1, keepdims=True) for y, x in zip(ys, nums)]
        grads = [(r * (y - x * (r * r * m))).astype(BF16) for r, y, x, m in zip(recips, ys, nums, inners)]
        sums = [mm(f, x, 0, 0) for f, x in zip(fqs, grads)]
        for k, j in enumerate(members[g]):
            put_head(r_tot, g, k, sums[2 * k] + sums[2 * k + 1])
            r_last[j] = sums[2 * k + 1]
        for (k, j, b), x, r, gr in zip(units(g), nums, recips, grads):
            att_ref[blocks[b], col(j)] = (x * r).astype(BF16)
            g_s[blocks[b], col(j)] = gr

    def adjoint_part(g):
        us = units(g)
        grads = [g_s[blocks[b], col(j)] for k, j, b in us]
        prefixes = [p_late[j] if b else get_head(p_chip, g, k) for k, j, b in us]
        backs = [mm(x, v_ref[blocks[b], col(j)], 1, 1) for x, (k, j, b) in zip(grads, us)]
        backs = [jnp.where(causal, x, 0.0).astype(BF16) for x in backs]
        gfqs = [mm(s, fk_s[blocks[b], col(j)], 1, 0) + mm(x, p, 1, 1)
                for s, (k, j, b), x, p in zip(backs, us, grads, prefixes)]
        fqs = [fq_s[blocks[b], col(j)] for k, j, b in us]
        gas = [(x * slope_of(f)).astype(BF16) for x, f in zip(gfqs, fqs)]
        qgs = [mm(x, w_ref[j], 1, 1).astype(BF16) for x, (k, j, b) in zip(gas, us)]
        wts = [mm(q_ref[blocks[b], col(j)], x, 0, 0) for x, (k, j, b) in zip(gas, us)]
        gfks = [mm(s, f, 0, 0) for s, f in zip(backs, fqs)]
        vgls = [mm(a_s[2 * j + b], x, 0, 0) for x, (k, j, b) in zip(grads, us)]
        for i, (k, j, b) in enumerate(us):
            qg_ref[blocks[b], col(j)] = qgs[i]
            gfk_s[blocks[b], col(j)] = gfks[i]
            vgl_s[blocks[b], col(j)] = vgls[i]
        for k, j in enumerate(members[g]):
            wt_s[j] = wts[2 * k] + wts[2 * k + 1]

    def key_part(g):
        for k, j in enumerate(members[g]):
            s_late[j] = (get_head(s_chip, g, k).astype(F32) + r_last[j]).astype(BF16)
        us = units(g)
        suffixes = [get_head(s_chip, g, k) if b else s_late[j] for k, j, b in us]
        gfks = [gfk_s[blocks[b], col(j)] + mm(v_ref[blocks[b], col(j)], s, 1, 1) for (k, j, b), s in zip(us, suffixes)]
        gbs = [(x * slope_of(fk_s[blocks[b], col(j)])).astype(BF16) for x, (k, j, b) in zip(gfks, us)]
        wts = [mm(k_ref[blocks[b], col(j)], x, 0, 0) for (k, j, b), x in zip(us, gbs)]
        for (k, j, b), x in zip(us, gbs):
            gb_s[blocks[b], col(j)] = x
        for k, j in enumerate(members[g]):
            whole = (wt_s[j] + (wts[2 * k] + wts[2 * k + 1])).astype(BF16)
            if shares == 1:
                f_tot[0, j] = whole
            else:
                for b in range(shares):
                    f_tot[b % 2, j * (shares // 2) + b // 2] = whole[b * rows:(b + 1) * rows]

    def send_rows(src, c):
        @pl.when(c != chip)
        def _():
            to_chip(4, 0, src, f_recv.at[chip], c).start()

        @pl.when(c == chip)
        def _():
            f_recv[chip] = src[...]

    def swap():
        return to_pair(f_tot.at[other], f_pair, f_pair_sems.at[0], f_pair_sems.at[1])

    def send_weights(g):
        if shares == 1:
            for j in members[g]:
                send_rows(f_tot.at[0, j], j)
        elif g == groups - 1:
            swap().start()
            swap().wait_recv()

            @pl.loop(0, held)
            def _(j):
                @pl.loop(0, shares // 2)
                def _(r):
                    at = j * (shares // 2) + r
                    send_rows(f_tot.at[core, at], (2 * j + core) * (shares // 2) + r)
                    send_rows(f_pair.at[at], (2 * j + other) * (shares // 2) + r)

    def last_part(g):
        us = units(g)
        suffixes = [get_head(s_chip, g, k) if b else s_late[j] for k, j, b in us]
        vgs = [vgl_s[blocks[b], col(j)] + mm(fk_s[blocks[b], col(j)], s, 1, 0) for (k, j, b), s in zip(us, suffixes)]
        kgs = [mm(gb_s[:, col(j)], w_ref[j], 1, 1) for j in members[g]]
        for (k, j, b), x in zip(us, vgs):
            vg_ref[blocks[b], col(j)] = x.astype(BF16)
        for k, j in enumerate(members[g]):
            kg_ref[:, col(j)] = kgs[k].astype(BF16)

    class Steps:
        def U(g):
            if g == 0:
                pl.semaphore_wait(barrier, jnp.where(is_owner, owners, owners + 1))
                for i in range(groups):
                    for j in members[i]:
                        give(0, j).start()
                        give(1, j).start()
            for j in members[g]:
                load_map(j).wait()
            ready(0, g)
            ready(1, g)
            state(g)
            to_owners(0, g, u_tot, u_recv)
            if g == 0:
                for j in range(held):
                    give(2, j).start()
            if g == groups - 1:
                for j in range(held):
                    give(3, j).start()

        def L(g):
            ready(2, g)
            local_part(g)

        def S(g):
            scan(0, g, u_recv, p_send, p_chip, lambda i: i)

        def N(g):
            ready(3, g)
            arrive(1, g, p_chip)
            numerators(g)
            to_owners(2, g, r_tot, r_recv)
            put_out(0, g)

        def A(g):
            adjoint_part(g)
            put_out(1, g)

        def RS(g):
            scan(2, g, r_recv, s_send, s_chip, lambda i: chips - 1 - i)

        def K(g):
            arrive(3, g, s_chip)
            key_part(g)
            send_weights(g)

        def E(g):
            last_part(g)
            put_out(2, g)
            put_out(3, g)

    for step in ORDER:
        name, g = step[:-1], int(step[-1])
        if g < groups:
            getattr(Steps, name)(g)

    some = f_recv.at[pl.ds(0, chips - 1)]
    to_chip(4, 0, some, some, some_chip()).wait_recv()

    def collect(c, acc):
        return acc + f_recv[c].astype(F32)

    fg_ref[...] = lax.fori_loop(0, chips, collect, jnp.zeros((rows, dh), F32), unroll=short) * scale

    for which in range(4):
        for j in range(held):
            store(which, j).wait()
        block = results[which][0].at[pl.ds(0, tokens)]
        both = to_pair(block, block, out_give_sems.at[which], out_take_sems.at[which])
        both.wait_send()
        both.wait_recv()
        to_pair(block, block, give_sems.at[which], out_take_sems.at[which]).wait_send()

    @pl.when(is_owner)
    def _():
        for phase, tot, send in ((0, u_tot, p_send), (2, r_tot, s_send)):
            sent = tot.at[:, pl.ds(0, owners - 1)]
            to_chip(phase, 0, sent, sent, some_chip()).wait_send()
            sent = send.at[:, pl.ds(0, chips - 1)]
            to_chip(phase + 1, 0, sent, sent, some_chip()).wait_send()

    @pl.when(jnp.logical_not(is_owner))
    def _():
        for phase, tot in ((0, u_tot), (2, r_tot)):
            to_chip(phase, 0, tot, tot, some_chip()).wait_send()

    to_chip(4, 0, some, some, some_chip()).wait_send()
    if shares > 1:
        swap().wait_send()


def copy_out(*refs):
    writes = [pltpu.make_async_copy(refs[i], refs[5 + i], refs[10].at[i]) for i in range(5)]
    for write in writes:
        write.start()
    for write in writes:
        write.wait()


def local(queries, keys, values, feature_map, out_grad):
    tokens, width = queries.shape
    heads, dh, _ = feature_map.shape
    n = lax.axis_size("seq")
    chips, rows, held = n // 2, heads * dh // n, heads // 2
    owners = chips // 2
    groups = max(1, min(GROUPS, held * dh // (owners * 16)))
    piece = held // groups * dh // owners
    slots = held * max(2, dh // rows) // 2
    wide = jax.ShapeDtypeStruct((tokens, width), BF16)
    vmem = pl.BlockSpec(memory_space=pltpu.VMEM)
    hbm = pl.BlockSpec(memory_space=pltpu.HBM)
    shapes = (wide, wide, wide, wide, jax.ShapeDtypeStruct((rows, dh), F32))
    outs = pl.pallas_call(
        functools.partial(kernel, n, heads, dh, groups, 1.0 / math.sqrt(tokens * n)),
        out_shape=(wide, pltpu.VMEM(wide.shape, BF16), pltpu.VMEM(wide.shape, BF16), pltpu.VMEM(wide.shape, BF16), shapes[4]),
        in_specs=[hbm] * 5,
        out_specs=(hbm, vmem, vmem, vmem, vmem),
        scratch_shapes=[pltpu.VMEM((2 * tokens, width // 2), BF16)] * 12 + [
            pltpu.VMEM((2 * tokens, width // 2), F32)] * 3 + [
            pltpu.VMEM((heads, tokens, tokens), BF16)] + [
            pltpu.VMEM((held, dh, dh), BF16)] * 3 + [
            pltpu.VMEM((held, dh, dh), F32)] * 3 + [
            pltpu.VMEM((groups, owners, piece, dh), BF16)] * 4 + [
            pltpu.VMEM((groups, chips, piece, dh), BF16)] * 4 + [
            pltpu.VMEM((2, slots, rows, dh), BF16),
            pltpu.VMEM((slots, rows, dh), BF16),
            pltpu.VMEM((chips, rows, dh), BF16),
            pltpu.SemaphoreType.DMA((5, held)),
            pltpu.SemaphoreType.DMA((4,)),
            pltpu.SemaphoreType.DMA((4, held)),
            pltpu.SemaphoreType.DMA((4, held)),
            pltpu.SemaphoreType.DMA((4,)),
            pltpu.SemaphoreType.DMA((4,)),
            pltpu.SemaphoreType.DMA((5,)),
            pltpu.SemaphoreType.DMA((5, groups)),
            pltpu.SemaphoreType.DMA((2,)),
        ],
        compiler_params=pltpu.CompilerParams(
            collective_id=0, has_side_effects=True, vmem_limit_bytes=40 << 20),
        name="linear_attention",
    )(*[pltpu.with_memory_space_constraint(x, pltpu.HBM) for x in (queries, keys, values, feature_map, out_grad)])
    outs = [pltpu.with_memory_space_constraint(x, pltpu.VMEM) if i in DIRECT else x for i, x in enumerate(outs)]
    outs = pl.pallas_call(
        copy_out,
        out_shape=shapes,
        in_specs=[vmem if i in DIRECT else pl.BlockSpec(memory_space=pl.ANY) for i in range(5)],
        out_specs=(hbm,) * 5,
        scratch_shapes=[pltpu.SemaphoreType.DMA((5,))],
        compiler_params=pltpu.CompilerParams(vmem_limit_bytes=16 << 20),
        name="copy_out",
    )(*outs)
    return tuple(outs[:4]) + (outs[4].reshape(rows * dh),)


def solution(mesh):
    wide = P(("grp", "seq"), None)
    return jax.shard_map(
        local, mesh=mesh, in_specs=(wide, wide, wide, P(), wide),
        out_specs=(wide, wide, wide, wide, P(("grp", "seq"))), check_vma=False)
```
